32 devices in a mesh: rep: 4 (over z), fsdp: 8 (over y, x, core).
Axes of the slice: x: 2, y: 2, z: 4, core: 2. Of those that a mesh axis runs over, the one named last changes fastest.
Arguments:
- activations: bfloat16 [4, 16384, 4096], P('rep', 'fsdp'), may hold values from -6 to 6
- cotangent: bfloat16 [4, 16384, 1024], P('rep', 'fsdp'), may hold values from -0.046875 to 0.046875
- momentum: float32 [4, 4096, 1024], P('rep', 'fsdp'), may hold values from -6 to 6
Outputs:
- momentum_next: float32 [4, 4096, 1024], P('rep', 'fsdp')
- update: float32 [4096, 1024], P('fsdp')
The draws below stay inside these ranges and needn't reach their ends.
All inputs are finite; a program needn't handle non-finite values.
Results may differ from the reference program's by a relative error of at most 0.0021.
Values sent between devices are 32-bit elements; how exact they have to be, the bound alone decides.
No kernel may reach another device: no remote copies, remote signals or barrier semaphores. Data moves between devices by JAX's collectives and lax.ppermute only.
A program may use at most 128 MiB of HBM per device.

```python
import jax
import jax.numpy as jnp
from jax import lax

D = 4096
KVW = 1024
TOK_DEV = 2048
CH = 64
BAND = 16
TOKENS = 16384
N_REP = 4
N_FSDP = 8


def levels(own_key, extent, pieces, low, high):
    loudness = 1.0
    for dim, shards_of in pieces:
        draws = jax.random.uniform(jax.random.fold_in(jax.random.fold_in(own_key, 6), dim), (shards_of,), jnp.float32, low / len(pieces), high / len(pieces))
        loudness = loudness * jnp.repeat(jnp.exp(draws), extent[dim] // shards_of).reshape((-1,) + (1,) * (len(extent) - 1 - dim))
    return loudness


def gaussian(key, shape, deviation, bound, pieces=(), kind=jnp.bfloat16):
    entries = jax.random.normal(key, shape, jnp.float32) * deviation
    if len(pieces) > 0:
        entries = levels(key, shape, pieces, -0.22, 0.18) * entries
    return jnp.clip(entries, min=-bound, max=bound).astype(kind)


def setup_inputs(seed: int = 0) -> dict:
    seeds = jax.random.split(jax.random.key(seed), 4)
    return {
        "activations": gaussian(seeds[0], (N_REP, TOKENS, D), 1.0, 6.0, ((0, 4), (1, 8))),
        "cotangent": gaussian(seeds[1], (N_REP, TOKENS, KVW), ((TOK_DEV * N_FSDP) ** -0.5), 0.046875, ((0, 4), (1, 8))),
        "momentum": gaussian(seeds[2], (N_REP, D, KVW), 1.0, 6.0, ((0, 4), (1, 8)), jnp.float32),
    }


momentum_decay = 0.9

def basis_rows(size, keep):
    freq = jnp.arange(keep, dtype=jnp.float32)[:, None]
    point = jnp.arange(size, dtype=jnp.float32)[None, :]
    waves = jnp.cos(jnp.pi * (2.0 * point + 1.0) * freq / (2.0 * size))
    scales = jnp.where(freq == 0.0, jnp.sqrt(1.0 / size), jnp.sqrt(2.0 / size))
    return (waves * scales).astype(jnp.float32)

def bands_of(field, basis):
    rows, width = field.shape
    blocks = field.reshape(rows // CH, CH, width // CH, CH)
    return jnp.einsum('kn,anbm,lm->akbl', basis, blocks, basis, precision=lax.Precision.HIGHEST)

def expand(bands, basis):
    count, _, wide, _ = bands.shape
    blocks = jnp.einsum('kn,akbl,lm->anbm', basis, bands, basis, precision=lax.Precision.HIGHEST)
    return blocks.reshape(count * CH, wide * CH)

def reference(activations, cotangent, momentum):
    basis = basis_rows(CH, BAND)
    nexts = []
    total = jnp.zeros((D, KVW), jnp.float32)
    for replica in range(N_REP):
        values = activations[replica].astype(jnp.float32)
        stat = lax.optimization_barrier(jnp.mean(values * values, axis=-1, keepdims=True))
        normed = (values * lax.rsqrt(stat + 1e-05)).astype(jnp.bfloat16)
        grad = lax.dot_general(normed, cotangent[replica], (((0,), (0,)), ((), ())), preferred_element_type=jnp.float32)
        accumulated = momentum_decay * momentum[replica] + grad
        component = expand(bands_of(accumulated, basis), basis)
        nexts.append(accumulated - component)
        total = total + component
    return (jnp.stack(nexts), total / N_REP)
```

```python
import jax
import jax.numpy as jnp
import numpy as np
from jax import lax
from jax.experimental import pallas as pl
from jax.experimental.pallas import tpu as pltpu
from jax.sharding import PartitionSpec as P

CH = 64
BAND = 16
EPS = 1e-05
ROWS = 128
SPAN = 512

momentum_decay = 0.9


def basis_rows(size, keep):
    freq = np.arange(keep, dtype=np.float64)[:, None]
    point = np.arange(size, dtype=np.float64)[None, :]
    waves = np.cos(np.pi * (2.0 * point + 1.0) * freq / (2.0 * size))
    scales = np.where(freq == 0.0, np.sqrt(1.0 / size), np.sqrt(2.0 / size))
    return (waves * scales).astype(np.float32)


def halves(value):
    high = value.astype(jnp.bfloat16)
    return high, (value - high.astype(jnp.float32)).astype(jnp.bfloat16)


def times_const(value, const):
    high, low = halves(value)
    return jnp.dot(
        jnp.concatenate([high, low, high], axis=1), const, preferred_element_type=jnp.float32
    )


def const_times(const, value):
    high, low = halves(value)
    return jnp.dot(
        const, jnp.concatenate([high, low, high], axis=0), preferred_element_type=jnp.float32
    )


def constants():
    small = basis_rows(CH, BAND)
    left = np.kron(np.eye(ROWS // CH, dtype=np.float32), small)
    right = np.kron(np.eye(SPAN // CH, dtype=np.float32), small.T)

    def split(m, axis, first):
        high, low = halves(jnp.asarray(m))
        parts = [high, high, low]
        return jnp.concatenate(parts, axis=axis)

    return {
        "bands_left": split(left, 1, True),
        "bands_right": split(right, 0, False),
        "expand_left": split(left.T, 1, True),
        "expand_right": split(right.T, 0, False),
    }


def bands_of(fields, left, right):
    tall = times_const(jnp.concatenate(fields, axis=0), right)
    wide = jnp.concatenate([tall[k * ROWS : (k + 1) * ROWS] for k in range(len(fields))], axis=1)
    return const_times(left, wide)


def expand(bands, left, right):
    low = ROWS * BAND // CH
    part = SPAN * BAND // CH
    spans = bands.shape[1] // part
    count = bands.shape[0]
    tall = times_const(
        jnp.concatenate([bands[:, s * part : (s + 1) * part] for s in range(spans)], axis=0), right
    )
    wide = jnp.concatenate([tall[s * count : (s + 1) * count] for s in range(spans)], axis=1)
    return [const_times(left, wide[k : k + low]) for k in range(0, count, low)]


def cost(flops, nbytes):
    return pl.CostEstimate(flops=int(flops), bytes_accessed=int(nbytes), transcendentals=0)


ANY = pl.BlockSpec(memory_space=pl.ANY)


def whole(array):
    return pl.BlockSpec(array.shape, lambda *_: (0,) * array.ndim)


def normed(x, scale):
    return (x.astype(jnp.float32) * scale).astype(jnp.bfloat16)


def transposed_dot(a, b):
    return lax.dot_general(a, b, (((0,), (0,)), ((), ())), preferred_element_type=jnp.float32)


def first_call(x, c, owners, n, rows, off, r, tile):
    tokens, width = x.shape
    cols = c.shape[1]
    half = n // 2
    group = 64

    def kernel(own, x_ref, c_ref, s_ref, p_ref):
        for g in range(0, tile, group):
            total = jnp.zeros((group, 128), jnp.float32)
            for s in range(0, width, 128):
                v = x_ref[g : g + group, s : s + 128].astype(jnp.float32)
                total = total + v * v
            stat = jnp.sum(total, axis=1, keepdims=True) / width
            s_ref[g : g + group, :] = jnp.broadcast_to(lax.rsqrt(stat + EPS), (group, 128))
        scale = s_ref[...]
        parts = []
        for j in range(half):
            at = pl.multiple_of(own[2 * j + 1] * rows + off, 128)
            parts.append(normed(x_ref[:, pl.ds(at, r)], scale))
        term = transposed_dot(jnp.concatenate(parts, axis=1), c_ref[...]).reshape(half, r, cols)

        @pl.when(pl.program_id(0) == 0)
        def _():
            p_ref[...] = term

        @pl.when(pl.program_id(0) > 0)
        def _():
            p_ref[...] += term

    return pl.pallas_call(
        kernel,
        out_shape=(
            jax.ShapeDtypeStruct((tokens, 128), jnp.float32),
            jax.ShapeDtypeStruct((half, r, cols), jnp.float32),
        ),
        grid_spec=pltpu.PrefetchScalarGridSpec(
            num_scalar_prefetch=1,
            grid=(tokens // tile,),
            in_specs=[
                pl.BlockSpec((tile, width), lambda i, own: (i, 0)),
                pl.BlockSpec((tile, cols), lambda i, own: (i, 0)),
            ],
            out_specs=(
                pl.BlockSpec((tile, 128), lambda i, own: (i, 0)),
                pl.BlockSpec((half, r, cols), lambda i, own: (0, 0, 0)),
            ),
        ),
        cost_estimate=cost(2 * tokens * half * r * cols, 2 * tokens * (width + cols)),
        name="first",
    )(owners, x, c)


def fill(xt_ref, x_refs, scale, r):
    for j, ref in enumerate(x_refs):
        xt_ref[j * r : (j + 1) * r, :] = normed(ref[...], scale).T


def product_specs(x, n, rows, off, r, parity, wide):
    tokens = x.shape[0]
    return [
        pl.BlockSpec((tokens, r), lambda h, own, j=j: (0, own[2 * j + parity] * (rows // r) + off // r))
        for j in range(n // 2)
    ] + [
        pl.BlockSpec((tokens, 128), lambda h, own: (0, 0)),
        pl.BlockSpec((tokens, wide), lambda h, own: (0, h)),
    ]


def product_call(x, scale, c, owners, n, rows, off, r, parity, deps):
    tokens = x.shape[0]
    cols = c.shape[1]
    half = n // 2
    wide = cols // 2

    def kernel(own, *refs):
        s_ref, c_ref = refs[half : half + 2]
        out_ref, xt_ref = refs[-2:]

        @pl.when(pl.program_id(0) == 0)
        def _():
            fill(xt_ref, refs[:half], s_ref[...], r)

        out_ref[...] = jnp.dot(
            xt_ref[...], c_ref[...], preferred_element_type=jnp.float32
        ).reshape(half, r, wide)

    return pl.pallas_call(
        kernel,
        out_shape=jax.ShapeDtypeStruct((half, r, cols), jnp.float32),
        grid_spec=pltpu.PrefetchScalarGridSpec(
            num_scalar_prefetch=1,
            grid=(2,),
            in_specs=product_specs(x, n, rows, off, r, parity, wide) + [ANY] * len(deps),
            out_specs=pl.BlockSpec((half, r, wide), lambda h, own: (0, 0, h)),
            scratch_shapes=[pltpu.VMEM((half * r, tokens), jnp.bfloat16)],
        ),
        cost_estimate=cost(2 * tokens * half * r * cols, 2 * tokens * (half * r + cols) + 4 * half * r * cols),
        name="product",
    )(owners, *[x] * half, scale, c, *deps)


def merge_call(x, scale, c, got, owners, n, rows, off, r, sends, keeps, deps):
    tokens = x.shape[0]
    cols = c.shape[1]
    half = n // 2
    wide = cols // 2

    def kernel(own, *refs):
        s_ref, c_ref, got_ref = refs[half : half + 3]
        outs, xt_ref = refs[-5:-1], refs[-1]

        @pl.when(pl.program_id(0) == 0)
        def _():
            fill(xt_ref, refs[:half], s_ref[...], r)

        total = jnp.dot(xt_ref[...], c_ref[...], preferred_element_type=jnp.float32)
        for side in range(2):

            @pl.when(pl.program_id(0) == side)
            def _():
                for out, masks in ((outs[2 * side], sends[side]), (outs[2 * side + 1], keeps[side])):
                    for k, m in enumerate(masks):
                        j = m // 2
                        out[k] = total[j * r : (j + 1) * r] + got_ref[j]

    shapes = [len(m) for side in range(2) for m in (sends[side], keeps[side])]
    return pl.pallas_call(
        kernel,
        out_shape=tuple(jax.ShapeDtypeStruct((k, r, wide), jnp.float32) for k in shapes),
        grid_spec=pltpu.PrefetchScalarGridSpec(
            num_scalar_prefetch=1,
            grid=(2,),
            in_specs=product_specs(x, n, rows, off, r, 0, wide)
            + [pl.BlockSpec((half, r, wide), lambda h, own: (0, 0, h))]
            + [ANY] * len(deps),
            out_specs=tuple(pl.BlockSpec((k, r, wide), lambda h, own: (0, 0, 0)) for k in shapes),
            scratch_shapes=[pltpu.VMEM((half * r, tokens), jnp.bfloat16)],
        ),
        cost_estimate=cost(2 * tokens * half * r * cols, 2 * tokens * (half * r + cols) + 8 * half * r * cols),
        name="merge",
    )(owners, *[x] * half, scale, c, got, *deps)


def stage_call(sends, r, wide, deps):
    specs, arrays, plan = [], [], []
    for terms_of in sends:
        plan.append([len(terms) for terms in terms_of])
        for terms in terms_of:
            for array, at in terms:
                arrays.append(array)
                specs.append(pl.BlockSpec((1, CH, wide), lambda i, at=at: (at, i, 0)))

    def kernel(*refs):
        outs = refs[len(arrays) + len(deps) :]
        k = 0
        for out, blocks in zip(outs, plan):
            for j, count in enumerate(blocks):
                total = refs[k][0]
                for e in range(1, count):
                    total = total + refs[k + e][0]
                out[j] = total
                k += count

    return pl.pallas_call(
        kernel,
        out_shape=tuple(jax.ShapeDtypeStruct((len(b), r, wide), jnp.float32) for b in plan),
        grid=(r // CH,),
        in_specs=specs + [ANY] * len(deps),
        out_specs=tuple(pl.BlockSpec((len(b), CH, wide), lambda i: (0, i, 0)) for b in plan),
        cost_estimate=cost(len(arrays) * r * wide, 6 * len(arrays) * r * wide),
        name="stage",
    )(*arrays, *deps)


def last_call(sends, keeps, momentum, consts, off, rows, wide, slot, slots, payload, before, deps):
    arrays, specs, counts = [], [], []
    r = ROWS
    for terms in sends + keeps:
        counts.append(len(terms))
        for array, at in terms:
            arrays.append(array)
            specs.append(pl.BlockSpec((1, r, wide), lambda i, at=at: (at, 0, 0)))
    base = off // r
    first = len(arrays)
    cols = 2 * wide
    left, right = consts["bands_left"], consts["bands_right"]
    arrays += [momentum, left, right]
    specs += [pl.BlockSpec((1, r, cols), lambda i: (0, base, 0)), whole(left), whole(right)]
    aliases = {}
    for old, outs in ((payload, (0, 1)), (before, (2, 3, 4, 5))):
        if old is not None:
            for array, out in zip(old, outs):
                aliases[len(arrays)] = out
                arrays.append(array)
                specs.append(ANY)
    arrays += list(deps)
    specs += [ANY] * len(deps)
    narrow = wide * BAND // CH
    low = r * BAND // CH

    def kernel(*refs):
        a_ref, b_ref, l_ref, ba_ref, bb_ref, bl_ref = refs[len(arrays) :]
        m_ref, left_ref, right_ref = refs[first : first + 3]
        k = 0
        sums = []
        for count in counts:
            total = refs[k][0]
            for e in range(1, count):
                total = total + refs[k + e][0]
            sums.append(total)
            k += count
        for side in range(2):
            at = slice(side * wide, (side + 1) * wide)
            sums[2 + side] = sums[2 + side] + momentum_decay * m_ref[0, :, at]
            l_ref[:, at] = sums[2 + side]
        a_ref[0] = sums[0]
        b_ref[0] = sums[1]
        spans = wide // SPAN
        fields = [total[:, s * SPAN : (s + 1) * SPAN] for total in sums for s in range(spans)]
        bands = bands_of(fields, left_ref[...], right_ref[...])
        ba_ref[...] = bands[:, :narrow]
        bb_ref[...] = bands[:, narrow : 2 * narrow]
        bl_ref[...] = bands[:, 2 * narrow :]

    high = rows * BAND // CH
    f32 = jnp.float32
    return pl.pallas_call(
        kernel,
        out_shape=(
            jax.ShapeDtypeStruct((slots, r, wide), f32),
            jax.ShapeDtypeStruct((slots, r, wide), f32),
            jax.ShapeDtypeStruct((rows, cols), f32),
            jax.ShapeDtypeStruct((high, narrow), f32),
            jax.ShapeDtypeStruct((high, narrow), f32),
            jax.ShapeDtypeStruct((high, 2 * narrow), f32),
        ),
        grid=(1,),
        in_specs=specs,
        out_specs=(
            pl.BlockSpec((1, r, wide), lambda i: (slot, 0, 0)),
            pl.BlockSpec((1, r, wide), lambda i: (slot, 0, 0)),
            pl.BlockSpec((r, cols), lambda i: (base, 0)),
            pl.BlockSpec((low, narrow), lambda i: (base, 0)),
            pl.BlockSpec((low, narrow), lambda i: (base, 0)),
            pl.BlockSpec((low, 2 * narrow), lambda i: (base, 0)),
        ),
        input_output_aliases=aliases,
        cost_estimate=cost(12 * r * cols * 128, 4 * r * wide * 20),
        name="last",
    )(*arrays)


def join_call(own, a, b):
    narrow = a.shape[1]

    def kernel(own_ref, a_ref, b_ref, out_ref):
        out_ref[:, :narrow] = own_ref[:, :narrow] + a_ref[...]
        out_ref[:, narrow:] = own_ref[:, narrow:] + b_ref[...]

    return pl.pallas_call(
        kernel,
        out_shape=jax.ShapeDtypeStruct(own.shape, jnp.float32),
        cost_estimate=cost(own.size, own.size * 12),
        name="join",
    )(own, a, b)


def tree(terms):
    while len(terms) > 1:
        terms = [terms[k] + terms[k + 1] for k in range(0, len(terms), 2)]
    return terms[0]


def update_call(bands, consts, rows, cols, deps):
    count = len(bands)
    step = 2 * ROWS if rows % (2 * ROWS) == 0 else ROWS
    left, right = consts["expand_left"], consts["expand_right"]

    def kernel(*refs):
        out_ref = refs[-1]
        total = tree([ref[...] for ref in refs[:count]]) / count
        for k, piece in enumerate(expand(total, refs[count][...], refs[count + 1][...])):
            out_ref[k * ROWS : (k + 1) * ROWS, :] = piece

    wide = bands[0].shape[1]
    return pl.pallas_call(
        kernel,
        out_shape=jax.ShapeDtypeStruct((rows, cols), jnp.float32),
        grid=(rows // step,),
        in_specs=[pl.BlockSpec((step * BAND // CH, wide), lambda i: (i, 0))] * count
        + [whole(left), whole(right)]
        + [ANY] * len(deps),
        out_specs=pl.BlockSpec((step, cols), lambda i: (i, 0)),
        cost_estimate=cost(6 * rows * cols * 128, 4 * rows * cols),
        name="update",
    )(*bands, left, right, *deps)


def finish_call(own, a, b, bands, consts, off, before, deps):
    rows, cols = own.shape
    wide = cols // 2
    count = a.shape[0]
    base = off // ROWS
    left, right = consts["expand_left"], consts["expand_right"]
    arrays = [own, a, b, bands, left, right]
    specs = [
        pl.BlockSpec((ROWS, cols), lambda i: (base + i, 0)),
        pl.BlockSpec((1, ROWS, wide), lambda i: (i, 0, 0)),
        pl.BlockSpec((1, ROWS, wide), lambda i: (i, 0, 0)),
        pl.BlockSpec((ROWS * BAND // CH, bands.shape[1]), lambda i: (base + i, 0)),
        whole(left),
        whole(right),
    ]
    aliases = {}
    if before is not None:
        aliases = {len(arrays): 0}
        arrays.append(before)
        specs.append(ANY)
    arrays += list(deps)
    specs += [ANY] * len(deps)

    def kernel(own_ref, a_ref, b_ref, g_ref, left_ref, right_ref, *refs):
        out_ref = refs[-1]
        (taken,) = expand(g_ref[...], left_ref[...], right_ref[...])
        out_ref[0, :, :wide] = own_ref[:, :wide] + a_ref[0] - taken[:, :wide]
        out_ref[0, :, wide:] = own_ref[:, wide:] + b_ref[0] - taken[:, wide:]

    return pl.pallas_call(
        kernel,
        out_shape=jax.ShapeDtypeStruct((1, rows, cols), jnp.float32),
        grid=(count,),
        in_specs=specs,
        out_specs=pl.BlockSpec((1, ROWS, cols), lambda i: (0, base + i, 0)),
        input_output_aliases=aliases,
        cost_estimate=cost(6 * count * ROWS * cols * 128, 12 * count * ROWS * cols),
        name="finish",
    )(*arrays)


def fast_body(n, groups, activations, cotangent, momentum):
    x, c = activations[0], cotangent[0]
    tokens, width = x.shape
    cols = c.shape[1]
    rows = width // n
    wide = cols // 2
    consts = constants()
    owners = lax.axis_index("fsdp").astype(jnp.int32) ^ jnp.arange(n, dtype=jnp.int32)
    bits = [1 << b for b in range(1, n.bit_length() - 1)]
    orders = (bits, bits[::-1])
    evens = range(0, n, 2)
    sends = [[m for m in evens if m & order[0]] for order in orders]
    keeps = [[m for m in evens if not m & order[0]] for order in orders]

    def swap(value, bit, axis="fsdp", size=n):
        return lax.ppermute(value, axis, [(i, i ^ bit) for i in range(size)])

    offs = list(range(0, rows, ROWS))
    count = len(offs)
    scale, odd = first_call(x, c, owners, n, rows, offs[0], ROWS, min(256, tokens))
    token = scale
    got = [swap(odd, 1)]
    state = []
    for k, off in enumerate(offs):
        if k + 1 < count:
            odd = product_call(x, scale, c, owners, n, rows, offs[k + 1], ROWS, 1, [token])
            token = odd
            got.append(swap(odd, 1))
        outs = merge_call(x, scale, c, got[k], owners, n, rows, off, ROWS, sends, keeps, [token])
        token = outs[1]
        terms = []
        for side in range(2):
            back = swap(outs[2 * side], orders[side][0])
            terms.append({m: [(outs[2 * side + 1], j), (back, j)] for j, m in enumerate(keeps[side])})
        for stage in range(1, len(bits) - 1):
            now = [orders[side][stage] for side in range(2)]
            out = stage_call(
                [[terms[side][m] for m in sorted(terms[side]) if m & now[side]] for side in range(2)],
                ROWS, wide, [],
            )
            for side in range(2):
                back = swap(out[side], now[side])
                keep = [m for m in sorted(terms[side]) if not m & now[side]]
                terms[side] = {m: terms[side][m] + [(back, j)] for j, m in enumerate(keep)}
        state.append(terms)

    ends = [order[-1] for order in orders]
    before = None
    bulk = []
    plan = [[0], list(range(1, count))] if count > 1 else [[0]]
    for members in plan:
        payload = None
        for slot, k in enumerate(members):
            terms = state[k]
            *payload, own, ba, bb, bl = last_call(
                [terms[side][ends[side]] for side in range(2)],
                [terms[side][0] for side in range(2)],
                momentum, consts, offs[k], rows, wide, slot, len(members), payload, before, [token],
            )
            before = [own, ba, bb, bl]
        bulk.append(payload)
    band_a = swap(before[1], ends[0])
    band_b = swap(before[2], ends[1])
    moved = [(swap(a, ends[0]), swap(b, ends[1])) for a, b in bulk]
    mine = join_call(before[3], band_a, band_b)
    every = [mine] + [swap(mine, k, "rep", groups) for k in range(1, groups)]
    update = update_call(every, consts, rows, cols, [])
    nexts = None
    for members, (a, b) in zip(plan, moved):
        nexts = finish_call(before[0], a, b, mine, consts, offs[members[0]], nexts, [])
    return nexts, update


def plain_body(n, groups, activations, cotangent, momentum):
    values = activations[0].astype(jnp.float32)
    stat = jnp.mean(values * values, axis=-1, keepdims=True)
    normed = (values * lax.rsqrt(stat + EPS)).astype(jnp.bfloat16)
    part = lax.dot_general(
        normed, cotangent[0], (((0,), (0,)), ((), ())), preferred_element_type=jnp.float32
    )
    basis = jnp.asarray(basis_rows(CH, BAND))
    grad = lax.psum_scatter(part, "fsdp", scatter_dimension=0, tiled=True)
    accumulated = momentum_decay * momentum[0] + grad
    rows, width = accumulated.shape
    blocks = accumulated.reshape(rows // CH, CH, width // CH, CH)
    high = lax.Precision.HIGHEST
    bands = jnp.einsum("kn,anbm,lm->akbl", basis, blocks, basis, precision=high)
    own = jnp.einsum("kn,akbl,lm->anbm", basis, bands, basis, precision=high)
    summed = lax.psum(bands, "rep")
    every = jnp.einsum("kn,akbl,lm->anbm", basis, summed, basis, precision=high)
    return ((accumulated - own.reshape(rows, width))[None], every.reshape(rows, width) / groups)


def power(k):
    return k & (k - 1) == 0


def solution(mesh):
    n, groups = mesh.shape["fsdp"], mesh.shape["rep"]

    def body(activations, cotangent, momentum):
        rows, cols = momentum.shape[1:]
        fits = power(n) and n >= 4 and power(groups)
        fits = fits and rows % ROWS == 0 and cols % (2 * SPAN) == 0 and activations.shape[1] % 256 == 0
        return (fast_body if fits else plain_body)(n, groups, activations, cotangent, momentum)

    return jax.shard_map(
        body,
        mesh=mesh,
        in_specs=(P("rep", "fsdp", None), P("rep", "fsdp", None), P("rep", "fsdp", None)),
        out_specs=(P("rep", "fsdp", None), P("fsdp", None)),
        check_vma=False,
    )
```

```python
import jax
import jax.numpy as jnp
import numpy as np
from jax import lax
from jax.experimental import pallas as pl
from jax.experimental.pallas import tpu as pltpu
from jax.sharding import PartitionSpec as P

CH = 64
BAND = 16
EPS = 1e-05
LATE = (5,)
ROWS = 128
SPAN = 256

momentum_decay = 0.9


def basis_rows(size, keep):
    freq = np.arange(keep, dtype=np.float64)[:, None]
    point = np.arange(size, dtype=np.float64)[None, :]
    waves = np.cos(np.pi * (2.0 * point + 1.0) * freq / (2.0 * size))
    scales = np.where(freq == 0.0, np.sqrt(1.0 / size), np.sqrt(2.0 / size))
    return (waves * scales).astype(np.float32)


def halves(value):
    high = value.astype(jnp.bfloat16)
    return high, (value - high.astype(jnp.float32)).astype(jnp.bfloat16)


def times_const(value, const):
    high, low = halves(value)
    return jnp.dot(
        jnp.concatenate([high, low, high], axis=1), const, preferred_element_type=jnp.float32
    )


def const_times(const, value):
    high, low = halves(value)
    return jnp.dot(
        const, jnp.concatenate([high, low, high], axis=0), preferred_element_type=jnp.float32
    )


def constants():
    small = basis_rows(CH, BAND)
    left = np.kron(np.eye(ROWS // CH, dtype=np.float32), small)
    right = np.kron(np.eye(SPAN // CH, dtype=np.float32), small.T)

    def split(m, axis):
        high, low = halves(jnp.asarray(m))
        parts = [high, high, low]
        return jnp.concatenate(parts, axis=axis)

    return {
        "bands_left": split(left, 1),
        "bands_right": split(right, 0),
        "expand_left": split(left.T, 1),
        "expand_right": split(right.T, 0),
    }


def bands_of(fields, left, right):
    tall = times_const(jnp.concatenate(fields, axis=0), right)
    wide = jnp.concatenate([tall[k * ROWS : (k + 1) * ROWS] for k in range(len(fields))], axis=1)
    return const_times(left, wide)


def expand(bands, left, right):
    low = ROWS * BAND // CH
    part = SPAN * BAND // CH
    spans = bands.shape[1] // part
    count = bands.shape[0]
    tall = times_const(
        jnp.concatenate([bands[:, s * part : (s + 1) * part] for s in range(spans)], axis=0), right
    )
    wide = jnp.concatenate([tall[s * count : (s + 1) * count] for s in range(spans)], axis=1)
    return [const_times(left, wide[k : k + low]) for k in range(0, count, low)]


def cost(flops, nbytes):
    return pl.CostEstimate(flops=int(flops), bytes_accessed=int(nbytes), transcendentals=0)


ANY = pl.BlockSpec(memory_space=pl.ANY)
VMEM = pl.BlockSpec(memory_space=pltpu.VMEM)
SMEM = pl.BlockSpec(memory_space=pltpu.SMEM)
F32 = jnp.float32


def on_chip(kernel, ins, tokens, outs, scratch=(), owners=None, flops=0, aliases=None, grant=12):
    lead = [] if owners is None else [owners]
    count = len(lead) + len(ins)

    def run(*refs):
        kernel(*refs[:count], *refs[count + len(tokens) :])

    arrays = [pltpu.with_memory_space_constraint(a, pltpu.VMEM) for a in [*ins, *tokens]]
    return pl.pallas_call(
        run,
        out_shape=tuple(pltpu.VMEM(shape, F32) for shape in outs),
        in_specs=[SMEM] * len(lead) + [VMEM] * len(arrays),
        out_specs=(VMEM,) * len(outs),
        scratch_shapes=list(scratch),
        input_output_aliases={len(lead) + i: o for i, o in (aliases or {}).items()},
        compiler_params=pltpu.CompilerParams(vmem_limit_bytes=grant << 20),
        cost_estimate=cost(flops, 0),
    )(*lead, *arrays)


def fill(xt_ref, x_ref, scale_ref, starts, r):
    scale = scale_ref[...]
    for j, at in enumerate(starts):
        piece = x_ref[:, pl.ds(pl.multiple_of(at, 128), r)].astype(F32) * scale
        xt_ref[j * r : (j + 1) * r, :] = piece.astype(jnp.bfloat16).T


def columns(side, cols, q, w):
    return slice(side * cols // 2 + q, side * cols // 2 + q + w)


def first_call(x, c, owners, n, rows, chunk):
    off, q, w = chunk
    r = ROWS
    tokens, width = x.shape
    cols = c.shape[1]
    half = n // 2
    tile = 128
    group = 64
    tiles = tokens // tile
    parts = [columns(side, cols, q, w) for side in range(2)]
    others = [
        slice(lo, hi)
        for side in range(2)
        for lo, hi in ((side * cols // 2, parts[side].start), (parts[side].stop, (side + 1) * cols // 2))
        if lo < hi
    ]

    def kernel(own, x_hbm, c_hbm, x_ref, c_ref, s_ref, p_ref, xt_ref, x_sem, c_sem):
        def piece(i):
            at = pl.ds(pl.multiple_of(i * tile, tile), tile)
            return pltpu.make_async_copy(x_hbm.at[at, :], x_ref.at[at, :], x_sem.at[i])

        def begin(i, _):
            piece(i).start()
            return 0

        def scale(i, _):
            piece(i).wait()
            for g in range(0, tile, group):
                at = pl.ds(pl.multiple_of(i * tile + g, group), group)
                total = jnp.zeros((group, 128), F32)
                for s in range(0, width, 128):
                    v = x_ref[at, s : s + 128].astype(F32)
                    total = total + v * v
                stat = jnp.sum(total, axis=1, keepdims=True) / width
                s_ref[at, :] = jnp.broadcast_to(lax.rsqrt(stat + EPS), (group, 128))
            return 0

        lax.fori_loop(0, tiles, begin, 0)
        rest = [
            pltpu.make_async_copy(c_hbm.at[:, at], c_ref.at[:, at], c_sem.at[k])
            for k, at in enumerate(parts + others)
        ]
        for copy in rest:
            copy.start()
        lax.fori_loop(0, tiles, scale, 0)
        fill(xt_ref, x_ref, s_ref, [own[2 * j + 1] * rows + off for j in range(half)], r)
        for side in range(2):
            rest[side].wait()
            p_ref[:, :, side * w : (side + 1) * w] = jnp.dot(
                xt_ref[...], c_ref[:, parts[side]], preferred_element_type=F32
            ).reshape(half, r, w)
        for copy in rest[2:]:
            copy.wait()

    return pl.pallas_call(
        kernel,
        out_shape=(
            pltpu.VMEM(x.shape, x.dtype),
            pltpu.VMEM(c.shape, c.dtype),
            pltpu.VMEM((tokens, 128), F32),
            pltpu.VMEM((half, r, 2 * w), F32),
        ),
        in_specs=[SMEM, ANY, ANY],
        out_specs=(VMEM,) * 4,
        scratch_shapes=[
            pltpu.VMEM((half * r, tokens), jnp.bfloat16),
            pltpu.SemaphoreType.DMA((tiles,)),
            pltpu.SemaphoreType.DMA((2 + len(others),)),
        ],
        compiler_params=pltpu.CompilerParams(vmem_limit_bytes=12 << 20),
        cost_estimate=cost(4 * tokens * half * r * w, 2 * tokens * (width + cols)),
        name="first",
    )(owners, *[pltpu.with_memory_space_constraint(a, pltpu.HBM) for a in (x, c)])


def product_call(x, scale, c, owners, n, rows, chunk, parity, tokens):
    off, q, w = chunk
    r = ROWS
    cols = c.shape[1]
    half = n // 2

    def kernel(own, x_ref, s_ref, c_ref, out_ref, xt_ref):
        fill(xt_ref, x_ref, s_ref, [own[2 * j + parity] * rows + off for j in range(half)], r)
        for side in range(2):
            out_ref[:, :, side * w : (side + 1) * w] = jnp.dot(
                xt_ref[...], c_ref[:, columns(side, cols, q, w)], preferred_element_type=F32
            ).reshape(half, r, w)

    (out,) = on_chip(
        kernel, [x, scale, c], tokens, [(half, r, 2 * w)],
        [pltpu.VMEM((half * r, x.shape[0]), jnp.bfloat16)], owners, 4 * x.shape[0] * half * r * w,
    )
    return out


def part_call(even, got, sends, keeps, tokens):
    r, w = even.shape[1], even.shape[2] // 2

    def kernel(even_ref, got_ref, *outs):
        for side in range(2):
            at = slice(side * w, (side + 1) * w)
            for out, masks in ((outs[2 * side], sends[side]), (outs[2 * side + 1], keeps[side])):
                for k, m in enumerate(masks):
                    out[k] = even_ref[m // 2, :, at] + got_ref[m // 2, :, at]

    shapes = [(len(m), r, w) for side in range(2) for m in (sends[side], keeps[side])]
    return on_chip(kernel, [even, got], tokens, shapes)


def add_up(terms, refs):
    total = None
    for array, at in terms:
        value = refs[array][at]
        total = value if total is None else total + value
    return total


def gather(groups):
    arrays, places = [], {}

    def place(array):
        if id(array) not in places:
            places[id(array)] = len(arrays)
            arrays.append(array)
        return places[id(array)]

    plan = [[[(place(a), at) for a, at in terms] for terms in group] for group in groups]
    return arrays, plan


def stage_call(sends, r, wide, tokens):
    arrays, plan = gather(sends)

    def kernel(*refs):
        for out, group in zip(refs[len(arrays) :], plan):
            for j, terms in enumerate(group):
                out[j] = add_up(terms, refs)

    return on_chip(kernel, arrays, tokens, [(len(g), r, wide) for g in plan])


def last_call(sends, keeps, momentum, consts, chunks, rows, wide, before, tokens):
    arrays, plan = gather([sends, keeps])
    terms = len(arrays)
    r = ROWS
    off, _, w = chunks[0]
    narrow = wide * BAND // CH
    low = r * BAND // CH
    high = rows * BAND // CH
    arrays = arrays + [momentum, consts["bands_left"], consts["bands_right"]]
    aliases = {}
    for k, array in enumerate(before or []):
        aliases[len(arrays)] = 2 + k
        arrays.append(array)
    count = len(arrays)
    subs = len(chunks)

    def kernel(*refs):
        out_refs = refs[count : count + 2]
        l_ref, ba_ref, bb_ref, bl_ref = refs[count + 2 :]
        m_ref, left_ref, right_ref = refs[terms : terms + 3]
        sums = [add_up(t, refs) for group in plan for t in group]
        for side in range(2):
            for k, (_, q, _) in enumerate(chunks):
                out_refs[side][k] = sums[side * subs + k]
                at = columns(side, 2 * wide, q, w)
                mine = sums[(2 + side) * subs + k] + momentum_decay * m_ref[0, off : off + r, at]
                sums[(2 + side) * subs + k] = mine
                l_ref[off : off + r, at] = mine
        fields = [total[:, s : s + SPAN] for total in sums for s in range(0, w, SPAN)]
        bands = bands_of(fields, left_ref[...], right_ref[...])
        at = slice(off * BAND // CH, off * BAND // CH + low)
        ba_ref[at, :] = bands[:, :narrow]
        bb_ref[at, :] = bands[:, narrow : 2 * narrow]
        bl_ref[at, :] = bands[:, 2 * narrow :]

    shapes = [
        (subs, r, w), (subs, r, w), (rows, 2 * wide),
        (high, narrow), (high, narrow), (high, 2 * narrow),
    ]
    return on_chip(kernel, arrays, tokens, shapes, flops=24 * r * wide * 128, aliases=aliases)


def join_call(own, a, b):
    narrow = a.shape[1]

    def kernel(own_ref, a_ref, b_ref, out_ref):
        out_ref[:, :narrow] = own_ref[:, :narrow] + a_ref[...]
        out_ref[:, narrow:] = own_ref[:, narrow:] + b_ref[...]

    return on_chip(kernel, [own, a, b], [], [own.shape])[0]


def tree(terms):
    while len(terms) > 1:
        terms = [terms[k] + terms[k + 1] for k in range(0, len(terms), 2)]
    return terms[0]


def outward(kernel, ins, tokens, shape, parts, part, flops, before=None):
    olds = [] if before is None else [before]

    def run(*refs):
        lead = refs[: len(ins)]
        out_hbm, buf, sem = refs[len(ins) + len(tokens) + len(olds) :]

        def send(k, index):
            pltpu.make_async_copy(buf.at[k], out_hbm.at[index], sem.at[k]).start()

        def wait(k, index):
            pltpu.make_async_copy(buf.at[k], out_hbm.at[index], sem.at[k]).wait()

        indices = kernel(buf, send, *lead)
        for k, index in enumerate(indices):
            wait(k, index)

    arrays = [pltpu.with_memory_space_constraint(a, pltpu.VMEM) for a in [*ins, *tokens]]
    return pl.pallas_call(
        run,
        out_shape=jax.ShapeDtypeStruct(shape, F32),
        in_specs=[VMEM] * len(arrays) + [ANY] * len(olds),
        out_specs=ANY,
        scratch_shapes=[pltpu.VMEM((parts,) + part, F32), pltpu.SemaphoreType.DMA((parts,))],
        input_output_aliases={len(arrays): 0} if olds else {},
        compiler_params=pltpu.CompilerParams(vmem_limit_bytes=12 << 20),
        cost_estimate=cost(flops, 4 * parts * part[0] * part[1]),
    )(*arrays, *olds)


def update_call(bands, consts, rows, cols, tokens):
    count = len(bands)
    parts = rows // ROWS

    def kernel(buf, send, *refs):
        total = tree([ref[...] for ref in refs[:count]]) / count
        pieces = expand(total, refs[count][...], refs[count + 1][...])
        indices = [pl.ds(k * ROWS, ROWS) for k in range(parts)]
        for k, piece in enumerate(pieces):
            buf[k] = piece
            send(k, indices[k])
        return indices

    return outward(
        kernel, [*bands, consts["expand_left"], consts["expand_right"]], tokens,
        (rows, cols), parts, (ROWS, cols), 6 * rows * cols * 128,
    )


def finish_call(own, a, b, bands, consts, chunks, before, tokens):
    rows, cols = own.shape
    low = ROWS * BAND // CH
    off, _, w = chunks[0]

    def kernel(buf, send, own_ref, a_ref, b_ref, g_ref, left_ref, right_ref):
        picked = g_ref[off * BAND // CH : off * BAND // CH + low, :]
        (taken,) = expand(picked, left_ref[...], right_ref[...])
        for side, ref in enumerate((a_ref, b_ref)):
            for k, (_, q, _) in enumerate(chunks):
                at = columns(side, cols, q, w)
                buf[0, :, at] = own_ref[off : off + ROWS, at] + ref[k] - taken[:, at]
        index = (0, pl.ds(off, ROWS))
        send(0, index)
        return [index]

    return outward(
        kernel, [own, a, b, bands, consts["expand_left"], consts["expand_right"]], tokens,
        (1, rows, cols), 1, (ROWS, cols), 6 * ROWS * cols * 128, before,
    )


def chunks_of(rows, wide):
    offs = list(range(0, rows, ROWS))
    groups = []
    for k, off in enumerate(offs):
        w = wide // 2 if k < 2 else wide
        groups.append([(off, q, w) for q in range(0, wide, w)])
    return groups


def fast_body(n, groups, activations, cotangent, momentum):
    x, c = activations[0], cotangent[0]
    width = x.shape[1]
    cols = c.shape[1]
    rows = width // n
    wide = cols // 2
    consts = constants()
    owners = lax.axis_index("fsdp").astype(jnp.int32) ^ jnp.arange(n, dtype=jnp.int32)
    bits = [1 << b for b in range(1, n.bit_length() - 1)]
    orders = (bits, bits[::-1])
    evens = range(0, n, 2)
    sends = [[m for m in evens if m & order[0]] for order in orders]
    keeps = [[m for m in evens if not m & order[0]] for order in orders]

    def swap(value, bit, axis="fsdp", size=n):
        return lax.ppermute(value, axis, [(i, i ^ bit) for i in range(size)])

    row_groups = chunks_of(rows, wide)
    chunks = [chunk for group in row_groups for chunk in group]
    x, c, scale, odd = first_call(x, c, owners, n, rows, chunks[0])
    token = odd
    got = swap(odd, 1)
    state = []
    for k, chunk in enumerate(chunks):
        even = product_call(x, scale, c, owners, n, rows, chunk, 0, [token])
        token = even
        here = got
        if k + 1 < len(chunks) and k + 1 not in LATE:
            odd = product_call(x, scale, c, owners, n, rows, chunks[k + 1], 1, [token])
            token = odd
            got = swap(odd, 1)
        outs = part_call(even, here, sends, keeps, [token])
        token = outs[1]
        if k + 1 < len(chunks) and k + 1 in LATE:
            odd = product_call(x, scale, c, owners, n, rows, chunks[k + 1], 1, [token])
            token = odd
            got = swap(odd, 1)
        terms = []
        for side in range(2):
            back = swap(outs[2 * side], orders[side][0])
            terms.append({m: [(outs[2 * side + 1], j), (back, j)] for j, m in enumerate(keeps[side])})
        for stage in range(1, len(bits) - 1):
            now = [orders[side][stage] for side in range(2)]
            out = stage_call(
                [[terms[side][m] for m in sorted(terms[side]) if m & now[side]] for side in range(2)],
                ROWS, chunk[2], [],
            )
            for side in range(2):
                back = swap(out[side], now[side])
                keep = [m for m in sorted(terms[side]) if not m & now[side]]
                terms[side] = {m: terms[side][m] + [(back, j)] for j, m in enumerate(keep)}
        state.append(terms)

    ends = [order[-1] for order in orders]
    before = None
    bulk = []
    at = 0
    for group in row_groups:
        held = state[at : at + len(group)]
        at += len(group)
        a, b, *before = last_call(
            [terms[side][ends[side]] for side in range(2) for terms in held],
            [terms[side][0] for side in range(2) for terms in held],
            momentum, consts, group, rows, wide, before, [token],
        )
        token = a
        bulk.append((swap(a, ends[0]), swap(b, ends[1])))
    band_a = swap(before[1], ends[0])
    band_b = swap(before[2], ends[1])
    mine = join_call(before[3], band_a, band_b)
    every = [mine] + [swap(mine, k, "rep", groups) for k in range(1, groups)]
    nexts = None
    token = mine
    final = len(row_groups) - 1
    for g, group in enumerate(row_groups):
        if g == final:
            update = update_call(every, consts, rows, cols, [token])
        nexts = finish_call(before[0], *bulk[g], mine, consts, group, nexts, [])
    return nexts, update


def plain_body(n, groups, activations, cotangent, momentum):
    values = activations[0].astype(jnp.float32)
    stat = jnp.mean(values * values, axis=-1, keepdims=True)
    normed = (values * lax.rsqrt(stat + EPS)).astype(jnp.bfloat16)
    part = lax.dot_general(
        normed, cotangent[0], (((0,), (0,)), ((), ())), preferred_element_type=jnp.float32
    )
    basis = jnp.asarray(basis_rows(CH, BAND))
    grad = lax.psum_scatter(part, "fsdp", scatter_dimension=0, tiled=True)
    accumulated = momentum_decay * momentum[0] + grad
    rows, width = accumulated.shape
    blocks = accumulated.reshape(rows // CH, CH, width // CH, CH)
    high = lax.Precision.HIGHEST
    bands = jnp.einsum("kn,anbm,lm->akbl", basis, blocks, basis, precision=high)
    own = jnp.einsum("kn,akbl,lm->anbm", basis, bands, basis, precision=high)
    summed = lax.psum(bands, "rep")
    every = jnp.einsum("kn,akbl,lm->anbm", basis, summed, basis, precision=high)
    return ((accumulated - own.reshape(rows, width))[None], every.reshape(rows, width) / groups)


def power(k):
    return k & (k - 1) == 0


def solution(mesh):
    n, groups = mesh.shape["fsdp"], mesh.shape["rep"]
    fits = power(n) and n >= 4 and power(groups)

    def body(activations, cotangent, momentum):
        rows, cols = momentum.shape[1:]
        good = fits and rows % ROWS == 0 and cols % (4 * SPAN) == 0 and activations.shape[1] % 256 == 0
        return (fast_body if good else plain_body)(n, groups, activations, cotangent, momentum)

    return jax.shard_map(
        body,
        mesh=mesh,
        in_specs=(P("rep", "fsdp", None), P("rep", "fsdp", None), P("rep", "fsdp", None)),
        out_specs=(P("rep", "fsdp", None), P("fsdp", None)),
        check_vma=False,
    )
```

```python
import jax
import jax.numpy as jnp
import numpy as np
from jax import lax
from jax.experimental import pallas as pl
from jax.experimental.pallas import tpu as pltpu
from jax.sharding import PartitionSpec as P

CH = 64
BAND = 16
EPS = 1e-05
LATE = (1, 5)
ROWS = 128
SPAN = 256

momentum_decay = 0.9


def basis_rows(size, keep):
    freq = np.arange(keep, dtype=np.float64)[:, None]
    point = np.arange(size, dtype=np.float64)[None, :]
    waves = np.cos(np.pi * (2.0 * point + 1.0) * freq / (2.0 * size))
    scales = np.where(freq == 0.0, np.sqrt(1.0 / size), np.sqrt(2.0 / size))
    return (waves * scales).astype(np.float32)


def halves(value):
    high = value.astype(jnp.bfloat16)
    return high, (value - high.astype(jnp.float32)).astype(jnp.bfloat16)


def times_const(value, const):
    high, low = halves(value)
    return jnp.dot(
        jnp.concatenate([high, low, high], axis=1), const, preferred_element_type=jnp.float32
    )


def const_times(const, value):
    high, low = halves(value)
    return jnp.dot(
        const, jnp.concatenate([high, low, high], axis=0), preferred_element_type=jnp.float32
    )


def constants():
    small = basis_rows(CH, BAND)
    left = np.kron(np.eye(ROWS // CH, dtype=np.float32), small)
    right = np.kron(np.eye(SPAN // CH, dtype=np.float32), small.T)

    def split(m, axis):
        high, low = halves(jnp.asarray(m))
        parts = [high, high, low]
        return jnp.concatenate(parts, axis=axis)

    return {
        "bands_left": split(left, 1),
        "bands_right": split(right, 0),
        "expand_left": split(left.T, 1),
        "expand_right": split(right.T, 0),
    }


def bands_of(fields, left, right):
    tall = times_const(jnp.concatenate(fields, axis=0), right)
    wide = jnp.concatenate([tall[k * ROWS : (k + 1) * ROWS] for k in range(len(fields))], axis=1)
    return const_times(left, wide)


def expand(bands, left, right):
    low = ROWS * BAND // CH
    part = SPAN * BAND // CH
    spans = bands.shape[1] // part
    count = bands.shape[0]
    tall = times_const(
        jnp.concatenate([bands[:, s * part : (s + 1) * part] for s in range(spans)], axis=0), right
    )
    wide = jnp.concatenate([tall[s * count : (s + 1) * count] for s in range(spans)], axis=1)
    return [const_times(left, wide[k : k + low]) for k in range(0, count, low)]


def cost(flops, nbytes):
    return pl.CostEstimate(flops=int(flops), bytes_accessed=int(nbytes), transcendentals=0)


ANY = pl.BlockSpec(memory_space=pl.ANY)
VMEM = pl.BlockSpec(memory_space=pltpu.VMEM)
SMEM = pl.BlockSpec(memory_space=pltpu.SMEM)
F32 = jnp.float32


def on_chip(kernel, ins, tokens, outs, scratch=(), owners=None, flops=0, aliases=None, far=(), grant=12):
    lead = [] if owners is None else [owners]
    count = len(lead) + len(ins) + len(far)

    outs = [out if isinstance(out[0], tuple) else (out, F32) for out in outs]

    def run(*refs):
        kernel(*refs[:count], *refs[count + len(tokens) :])

    near = [pltpu.with_memory_space_constraint(a, pltpu.VMEM) for a in ins]
    past = [pltpu.with_memory_space_constraint(a, pltpu.VMEM) for a in tokens]
    far = [pltpu.with_memory_space_constraint(a, pltpu.HBM) for a in far]
    return pl.pallas_call(
        run,
        out_shape=tuple(pltpu.VMEM(shape, kind) for shape, kind in outs),
        in_specs=[SMEM] * len(lead) + [VMEM] * len(near) + [ANY] * len(far) + [VMEM] * len(past),
        out_specs=(VMEM,) * len(outs),
        scratch_shapes=list(scratch),
        input_output_aliases={len(lead) + i: o for i, o in (aliases or {}).items()},
        compiler_params=pltpu.CompilerParams(vmem_limit_bytes=grant << 20),
        cost_estimate=cost(flops, 0),
    )(*lead, *near, *far, *past)


def fill(xt_ref, x_ref, scale_ref, starts, r):
    scale = scale_ref[...]
    for j, at in enumerate(starts):
        piece = x_ref[:, pl.ds(pl.multiple_of(at, 128), r)].astype(F32) * scale
        xt_ref[j * r : (j + 1) * r, :] = piece.astype(jnp.bfloat16).T


def columns(side, cols, q, w):
    return slice(side * cols // 2 + q, side * cols // 2 + q + w)


def first_call(x, c, owners, n, rows, chunk):
    off, q, w = chunk
    r = ROWS
    tokens, width = x.shape
    cols = c.shape[1]
    half = n // 2
    tile = 256
    group = 64
    steps = tokens // tile
    parts = [columns(side, cols, q, w) for side in range(2)]

    def kernel(own, x_hbm, c_hbm, x_ref, c_ref, s_ref, p_ref, xt_ref, x_sem, c_sem):
        def rows_at(i):
            return pl.ds(pl.multiple_of(i * tile, tile), tile)

        def piece(i):
            at = rows_at(i)
            return pltpu.make_async_copy(x_hbm.at[at, :], x_ref.at[at, :], x_sem.at[i])

        def begin(i, _):
            piece(i).start()
            return 0

        def scales(i):
            out = []
            for g in range(0, tile, group):
                at = pl.ds(pl.multiple_of(i * tile + g, group), group)
                total = jnp.zeros((group, 128), F32)
                for s in range(0, width, 128):
                    v = x_ref[at, s : s + 128].astype(F32)
                    total = total + v * v
                stat = jnp.sum(total, axis=1, keepdims=True) / width
                out.append(jnp.broadcast_to(lax.rsqrt(stat + EPS), (group, 128)))
            return jnp.concatenate(out, axis=0)

        def turn(i, now):
            at = rows_at(i)
            for j in range(half):
                lanes = pl.ds(pl.multiple_of(own[2 * j + 1] * rows + off, 128), r)
                value = (x_ref[at, lanes].astype(F32) * now).astype(jnp.bfloat16)
                xt_ref[j * r : (j + 1) * r, at] = value.T

        def both(i, _):
            piece(i + 1).wait()
            now = s_ref[rows_at(i), :]
            later = scales(i + 1)
            turn(i, now)
            s_ref[rows_at(i + 1), :] = later
            return 0

        near = [
            pltpu.make_async_copy(c_hbm.at[:, at], c_ref.at[:, at], c_sem.at[side])
            for side, at in enumerate(parts)
        ]
        for copy in near:
            copy.start()
        lax.fori_loop(0, steps, begin, 0)
        piece(0).wait()
        s_ref[rows_at(0), :] = scales(0)
        lax.fori_loop(0, steps - 2, both, 0)
        for copy in near:
            copy.wait()
        cut = (steps - 2) * tile
        for side in range(2):
            p_ref[:, :, side * w : (side + 1) * w] = jnp.dot(
                xt_ref[:, :cut], c_ref[:cut, parts[side]], preferred_element_type=F32
            ).reshape(half, r, w)
        both(steps - 2, 0)
        turn(steps - 1, s_ref[rows_at(steps - 1), :])
        for side in range(2):
            p_ref[:, :, side * w : (side + 1) * w] += jnp.dot(
                xt_ref[:, cut:], c_ref[cut:, parts[side]], preferred_element_type=F32
            ).reshape(half, r, w)

    return pl.pallas_call(
        kernel,
        out_shape=(
            pltpu.VMEM(x.shape, x.dtype),
            pltpu.VMEM(c.shape, c.dtype),
            pltpu.VMEM((tokens, 128), F32),
            pltpu.VMEM((half, r, 2 * w), F32),
            pltpu.VMEM((half * r, tokens), jnp.bfloat16),
        ),
        in_specs=[SMEM, ANY, ANY],
        out_specs=(VMEM,) * 5,
        scratch_shapes=[
            pltpu.SemaphoreType.DMA((steps,)),
            pltpu.SemaphoreType.DMA((2,)),
        ],
        compiler_params=pltpu.CompilerParams(vmem_limit_bytes=12 << 20),
        cost_estimate=cost(4 * tokens * half * r * w, 2 * tokens * (width + cols)),
        name="first",
    )(owners, *[pltpu.with_memory_space_constraint(a, pltpu.HBM) for a in (x, c)])


def product_call(x, scale, c, owners, n, rows, chunk, parity, xt, tokens):
    off, q, w = chunk
    r = ROWS
    cols = c.shape[1]
    half = n // 2

    def multiply(xt_ref, c_ref, out_ref):
        for side in range(2):
            out_ref[:, :, side * w : (side + 1) * w] = jnp.dot(
                xt_ref[...], c_ref[:, columns(side, cols, q, w)], preferred_element_type=F32
            ).reshape(half, r, w)

    def kernel(own, x_ref, s_ref, c_ref, out_ref, xt_ref):
        fill(xt_ref, x_ref, s_ref, [own[2 * j + parity] * rows + off for j in range(half)], r)
        multiply(xt_ref, c_ref, out_ref)

    shape = (half, r, 2 * w)
    flops = 4 * x.shape[0] * half * r * w
    if xt is not None:
        (out,) = on_chip(multiply, [xt, c], tokens, [shape], flops=flops)
        return out, xt
    return on_chip(
        kernel, [x, scale, c], tokens,
        [shape, ((half * r, x.shape[0]), jnp.bfloat16)], owners=owners, flops=flops,
    )


def second_call(x, scale, c, c_hbm, owners, n, rows, chunk, tokens):
    off, q, w = chunk
    cols = c.shape[1]
    half = n // 2
    parts = [columns(side, cols, q, w) for side in range(2)]
    others = [
        slice(lo, hi)
        for side in range(2)
        for lo, hi in ((side * cols // 2, parts[side].start), (parts[side].stop, (side + 1) * cols // 2))
        if lo < hi
    ]

    def kernel(own, x_ref, s_ref, old_ref, from_ref, out_ref, c_ref, xt_ref, sem):
        rest = [
            pltpu.make_async_copy(from_ref.at[:, at], c_ref.at[:, at], sem.at[k])
            for k, at in enumerate(others)
        ]
        for copy in rest:
            copy.start()
        fill(xt_ref, x_ref, s_ref, [own[2 * j] * rows + off for j in range(half)], ROWS)
        for side in range(2):
            out_ref[:, :, side * w : (side + 1) * w] = jnp.dot(
                xt_ref[...], c_ref[:, parts[side]], preferred_element_type=F32
            ).reshape(half, ROWS, w)
        for copy in rest:
            copy.wait()

    return on_chip(
        kernel, [x, scale, c], tokens,
        [(half, ROWS, 2 * w), (c.shape, c.dtype), ((half * ROWS, x.shape[0]), x.dtype)],
        [pltpu.SemaphoreType.DMA((max(len(others), 1),))], owners, 4 * c.shape[0] * half * ROWS * w,
        aliases={2: 1}, far=[c_hbm],
    )


def part_call(even, got, sends, keeps, tokens):
    r, w = even.shape[1], even.shape[2] // 2

    def kernel(even_ref, got_ref, *outs):
        for side in range(2):
            at = slice(side * w, (side + 1) * w)
            for out, masks in ((outs[2 * side], sends[side]), (outs[2 * side + 1], keeps[side])):
                for k, m in enumerate(masks):
                    out[k] = even_ref[m // 2, :, at] + got_ref[m // 2, :, at]

    shapes = [(len(m), r, w) for side in range(2) for m in (sends[side], keeps[side])]
    return on_chip(kernel, [even, got], tokens, shapes)


def add_up(terms, refs):
    total = None
    for array, at in terms:
        value = refs[array][at]
        total = value if total is None else total + value
    return total


def gather(groups):
    arrays, places = [], {}

    def place(array):
        if id(array) not in places:
            places[id(array)] = len(arrays)
            arrays.append(array)
        return places[id(array)]

    plan = [[[(place(a), at) for a, at in terms] for terms in group] for group in groups]
    return arrays, plan


def stage_call(sends, r, wide, tokens):
    arrays, plan = gather(sends)

    def kernel(*refs):
        for out, group in zip(refs[len(arrays) :], plan):
            for j, terms in enumerate(group):
                out[j] = add_up(terms, refs)

    return on_chip(kernel, arrays, tokens, [(len(g), r, wide) for g in plan])


def last_call(sends, keeps, momentum, consts, chunks, rows, wide, before, tokens):
    arrays, plan = gather([sends, keeps])
    terms = len(arrays)
    r = ROWS
    off, _, w = chunks[0]
    narrow = wide * BAND // CH
    low = r * BAND // CH
    high = rows * BAND // CH
    arrays = arrays + [momentum, consts["bands_left"], consts["bands_right"]]
    aliases = {}
    for k, array in enumerate(before or []):
        aliases[len(arrays)] = 2 + k
        arrays.append(array)
    count = len(arrays)
    subs = len(chunks)

    def kernel(*refs):
        out_refs = refs[count : count + 2]
        l_ref, ba_ref, bb_ref, bl_ref = refs[count + 2 :]
        m_ref, left_ref, right_ref = refs[terms : terms + 3]
        sums = [add_up(t, refs) for group in plan for t in group]
        for side in range(2):
            for k, (_, q, _) in enumerate(chunks):
                out_refs[side][k] = sums[side * subs + k]
                at = columns(side, 2 * wide, q, w)
                mine = sums[(2 + side) * subs + k] + momentum_decay * m_ref[0, off : off + r, at]
                sums[(2 + side) * subs + k] = mine
                l_ref[off : off + r, at] = mine
        fields = [total[:, s : s + SPAN] for total in sums for s in range(0, w, SPAN)]
        bands = bands_of(fields, left_ref[...], right_ref[...])
        at = slice(off * BAND // CH, off * BAND // CH + low)
        ba_ref[at, :] = bands[:, :narrow]
        bb_ref[at, :] = bands[:, narrow : 2 * narrow]
        bl_ref[at, :] = bands[:, 2 * narrow :]

    shapes = [
        (subs, r, w), (subs, r, w), (rows, 2 * wide),
        (high, narrow), (high, narrow), (high, 2 * narrow),
    ]
    return on_chip(kernel, arrays, tokens, shapes, flops=24 * r * wide * 128, aliases=aliases)


def join_call(own, a, b):
    narrow = a.shape[1]

    def kernel(own_ref, a_ref, b_ref, out_ref):
        out_ref[:, :narrow] = own_ref[:, :narrow] + a_ref[...]
        out_ref[:, narrow:] = own_ref[:, narrow:] + b_ref[...]

    return on_chip(kernel, [own, a, b], [], [own.shape])[0]


def tree(terms):
    while len(terms) > 1:
        terms = [terms[k] + terms[k + 1] for k in range(0, len(terms), 2)]
    return terms[0]


def outward(kernel, ins, tokens, shape, parts, part, flops, before=None):
    olds = [] if before is None else [before]

    def run(*refs):
        lead = refs[: len(ins)]
        out_hbm, buf, sem = refs[len(ins) + len(tokens) + len(olds) :]

        def send(k, index):
            pltpu.make_async_copy(buf.at[k], out_hbm.at[index], sem.at[k]).start()

        def wait(k, index):
            pltpu.make_async_copy(buf.at[k], out_hbm.at[index], sem.at[k]).wait()

        indices = kernel(buf, send, *lead)
        for k, index in enumerate(indices):
            wait(k, index)

    arrays = [pltpu.with_memory_space_constraint(a, pltpu.VMEM) for a in [*ins, *tokens]]
    return pl.pallas_call(
        run,
        out_shape=jax.ShapeDtypeStruct(shape, F32),
        in_specs=[VMEM] * len(arrays) + [ANY] * len(olds),
        out_specs=ANY,
        scratch_shapes=[pltpu.VMEM((parts,) + part, F32), pltpu.SemaphoreType.DMA((parts,))],
        input_output_aliases={len(arrays): 0} if olds else {},
        compiler_params=pltpu.CompilerParams(vmem_limit_bytes=12 << 20),
        cost_estimate=cost(flops, 4 * parts * part[0] * part[1]),
    )(*arrays, *olds)


def update_call(bands, consts, rows, cols, tokens):
    count = len(bands)
    parts = rows // ROWS

    def kernel(buf, send, *refs):
        total = tree([ref[...] for ref in refs[:count]]) / count
        pieces = expand(total, refs[count][...], refs[count + 1][...])
        indices = [pl.ds(k * ROWS, ROWS) for k in range(parts)]
        for k, piece in enumerate(pieces):
            buf[k] = piece
            send(k, indices[k])
        return indices

    return outward(
        kernel, [*bands, consts["expand_left"], consts["expand_right"]], tokens,
        (rows, cols), parts, (ROWS, cols), 6 * rows * cols * 128,
    )


def settle_call(own, bands, consts, tokens):
    def kernel(own_ref, g_ref, left_ref, right_ref, out_ref):
        for k, taken in enumerate(expand(g_ref[...], left_ref[...], right_ref[...])):
            at = slice(k * ROWS, (k + 1) * ROWS)
            out_ref[at, :] = own_ref[at, :] - taken

    return on_chip(
        kernel, [own, bands, consts["expand_left"], consts["expand_right"]], tokens,
        [own.shape], flops=6 * own.size * 128, aliases={0: 0},
    )[0]


def finish_call(own, a, b, chunks, before, tokens):
    rows, cols = own.shape
    off, _, w = chunks[0]
    parts = 2
    step = ROWS // parts

    def kernel(buf, send, own_ref, a_ref, b_ref):
        indices = []
        for part in range(parts):
            lo = part * step
            for side, ref in enumerate((a_ref, b_ref)):
                for k, (_, q, _) in enumerate(chunks):
                    at = columns(side, cols, q, w)
                    buf[part, :, at] = own_ref[off + lo : off + lo + step, at] + ref[k, lo : lo + step]
            indices.append((0, pl.ds(off + lo, step)))
            send(part, indices[part])
        return indices

    return outward(kernel, [own, a, b], tokens, (1, rows, cols), parts, (step, cols), 0, before)


def chunks_of(rows, wide):
    offs = list(range(0, rows, ROWS))
    groups = []
    for k, off in enumerate(offs):
        w = wide // 2 if k < 2 else wide
        groups.append([(off, q, w) for q in range(0, wide, w)])
    return groups


def fast_body(n, groups, activations, cotangent, momentum):
    x, c = activations[0], cotangent[0]
    width = x.shape[1]
    cols = c.shape[1]
    rows = width // n
    wide = cols // 2
    consts = constants()
    owners = lax.axis_index("fsdp").astype(jnp.int32) ^ jnp.arange(n, dtype=jnp.int32)
    bits = [1 << b for b in range(1, n.bit_length() - 1)]
    orders = (bits, bits[::-1])
    evens = range(0, n, 2)
    sends = [[m for m in evens if m & order[0]] for order in orders]
    keeps = [[m for m in evens if not m & order[0]] for order in orders]

    def swap(value, bit, axis="fsdp", size=n):
        return lax.ppermute(value, axis, [(i, i ^ bit) for i in range(size)])

    row_groups = chunks_of(rows, wide)
    chunks = [chunk for group in row_groups for chunk in group]
    c_hbm = c
    x, c, scale, odd, xt = first_call(x, c, owners, n, rows, chunks[0])
    token = odd
    kept = {(1, chunks[0][0]): xt}

    def product(k, parity):
        at = parity, chunks[k][0]
        out, kept[at] = product_call(
            x, scale, c, owners, n, rows, chunks[k], parity, kept.get(at), [token]
        )
        return out

    got = swap(odd, 1)
    state = []
    for k, chunk in enumerate(chunks):
        if k == 0:
            even, c, kept[0, chunk[0]] = second_call(
                x, scale, c, c_hbm, owners, n, rows, chunk, [token]
            )
        else:
            even = product(k, 0)
        token = even
        here = got
        if k + 1 < len(chunks) and k + 1 not in LATE:
            odd = product(k + 1, 1)
            token = odd
            got = swap(odd, 1)
        outs = part_call(even, here, sends, keeps, [token])
        token = outs[1]
        if k + 1 < len(chunks) and k + 1 in LATE:
            odd = product(k + 1, 1)
            token = odd
            got = swap(odd, 1)
        terms = []
        for side in range(2):
            back = swap(outs[2 * side], orders[side][0])
            terms.append({m: [(outs[2 * side + 1], j), (back, j)] for j, m in enumerate(keeps[side])})
        for stage in range(1, len(bits) - 1):
            now = [orders[side][stage] for side in range(2)]
            out = stage_call(
                [[terms[side][m] for m in sorted(terms[side]) if m & now[side]] for side in range(2)],
                ROWS, chunk[2], [],
            )
            for side in range(2):
                back = swap(out[side], now[side])
                keep = [m for m in sorted(terms[side]) if not m & now[side]]
                terms[side] = {m: terms[side][m] + [(back, j)] for j, m in enumerate(keep)}
        state.append(terms)

    ends = [order[-1] for order in orders]
    before = None
    bulk = []
    at = 0
    for group in row_groups:
        held = state[at : at + len(group)]
        at += len(group)
        a, b, *before = last_call(
            [terms[side][ends[side]] for side in range(2) for terms in held],
            [terms[side][0] for side in range(2) for terms in held],
            momentum, consts, group, rows, wide, before, [token],
        )
        token = a
        bulk.append((swap(a, ends[0]), swap(b, ends[1])))
    band_a = swap(before[1], ends[0])
    band_b = swap(before[2], ends[1])
    mine = join_call(before[3], band_a, band_b)
    every = [mine] + [swap(mine, k, "rep", groups) for k in range(1, groups)]
    settled = settle_call(before[0], mine, consts, [])
    nexts = None
    final = len(row_groups) - 1
    for g, group in enumerate(row_groups):
        if g == final:
            update = update_call(every, consts, rows, cols, [settled])
        nexts = finish_call(settled, *bulk[g], group, nexts, [])
    return nexts, update


def plain_body(n, groups, activations, cotangent, momentum):
    values = activations[0].astype(jnp.float32)
    stat = jnp.mean(values * values, axis=-1, keepdims=True)
    normed = (values * lax.rsqrt(stat + EPS)).astype(jnp.bfloat16)
    part = lax.dot_general(
        normed, cotangent[0], (((0,), (0,)), ((), ())), preferred_element_type=jnp.float32
    )
    basis = jnp.asarray(basis_rows(CH, BAND))
    grad = lax.psum_scatter(part, "fsdp", scatter_dimension=0, tiled=True)
    accumulated = momentum_decay * momentum[0] + grad
    rows, width = accumulated.shape
    blocks = accumulated.reshape(rows // CH, CH, width // CH, CH)
    high = lax.Precision.HIGHEST
    bands = jnp.einsum("kn,anbm,lm->akbl", basis, blocks, basis, precision=high)
    own = jnp.einsum("kn,akbl,lm->anbm", basis, bands, basis, precision=high)
    summed = lax.psum(bands, "rep")
    every = jnp.einsum("kn,akbl,lm->anbm", basis, summed, basis, precision=high)
    return ((accumulated - own.reshape(rows, width))[None], every.reshape(rows, width) / groups)


def power(k):
    return k & (k - 1) == 0


def solution(mesh):
    n, groups = mesh.shape["fsdp"], mesh.shape["rep"]
    fits = power(n) and n >= 4 and power(groups)

    def body(activations, cotangent, momentum):
        rows, cols = momentum.shape[1:]
        good = fits and rows % ROWS == 0 and cols % (4 * SPAN) == 0 and activations.shape[1] % 512 == 0
        return (fast_body if good else plain_body)(n, groups, activations, cotangent, momentum)

    return jax.shard_map(
        body,
        mesh=mesh,
        in_specs=(P("rep", "fsdp", None), P("rep", "fsdp", None), P("rep", "fsdp", None)),
        out_specs=(P("rep", "fsdp", None), P("fsdp", None)),
        check_vma=False,
    )
```

```python
import jax
import jax.numpy as jnp
import numpy as np
from jax import lax
from jax.experimental import pallas as pl
from jax.experimental.pallas import tpu as pltpu
from jax.sharding import PartitionSpec as P

CH = 64
BAND = 16
EPS = 1e-05
LATE = (5,)
ROWS = 128
SPAN = 256

momentum_decay = 0.9


def basis_rows(size, keep):
    freq = np.arange(keep, dtype=np.float64)[:, None]
    point = np.arange(size, dtype=np.float64)[None, :]
    waves = np.cos(np.pi * (2.0 * point + 1.0) * freq / (2.0 * size))
    scales = np.where(freq == 0.0, np.sqrt(1.0 / size), np.sqrt(2.0 / size))
    return (waves * scales).astype(np.float32)


def halves(value):
    high = value.astype(jnp.bfloat16)
    return high, (value - high.astype(jnp.float32)).astype(jnp.bfloat16)


def times_const(value, const):
    high, low = halves(value)
    return jnp.dot(
        jnp.concatenate([high, low, high], axis=1), const, preferred_element_type=jnp.float32
    )


def const_times(const, value):
    high, low = halves(value)
    return jnp.dot(
        const, jnp.concatenate([high, low, high], axis=0), preferred_element_type=jnp.float32
    )


def constants():
    small = basis_rows(CH, BAND)
    left = np.kron(np.eye(ROWS // CH, dtype=np.float32), small)
    right = np.kron(np.eye(SPAN // CH, dtype=np.float32), small.T)

    def split(m, axis):
        high, low = halves(jnp.asarray(m))
        parts = [high, high, low]
        return jnp.concatenate(parts, axis=axis)

    return {
        "bands_left": split(left, 1),
        "bands_right": split(right, 0),
        "expand_left": split(left.T, 1),
        "expand_right": split(right.T, 0),
    }


def bands_of(fields, left, right):
    tall = times_const(jnp.concatenate(fields, axis=0), right)
    wide = jnp.concatenate([tall[k * ROWS : (k + 1) * ROWS] for k in range(len(fields))], axis=1)
    return const_times(left, wide)


def expand(bands, left, right):
    low = ROWS * BAND // CH
    part = SPAN * BAND // CH
    spans = bands.shape[1] // part
    count = bands.shape[0]
    tall = times_const(
        jnp.concatenate([bands[:, s * part : (s + 1) * part] for s in range(spans)], axis=0), right
    )
    wide = jnp.concatenate([tall[s * count : (s + 1) * count] for s in range(spans)], axis=1)
    return [const_times(left, wide[k : k + low]) for k in range(0, count, low)]


def cost(flops, nbytes):
    return pl.CostEstimate(flops=int(flops), bytes_accessed=int(nbytes), transcendentals=0)


ANY = pl.BlockSpec(memory_space=pl.ANY)
VMEM = pl.BlockSpec(memory_space=pltpu.VMEM)
SMEM = pl.BlockSpec(memory_space=pltpu.SMEM)
F32 = jnp.float32


def on_chip(kernel, ins, tokens, outs, scratch=(), owners=None, flops=0, aliases=None, far=(), grant=12):
    lead = [] if owners is None else [owners]
    count = len(lead) + len(ins) + len(far)

    outs = [out if isinstance(out[0], tuple) else (out, F32) for out in outs]

    def run(*refs):
        kernel(*refs[:count], *refs[count + len(tokens) :])

    near = [pltpu.with_memory_space_constraint(a, pltpu.VMEM) for a in ins]
    past = [pltpu.with_memory_space_constraint(a, pltpu.VMEM) for a in tokens]
    far = [pltpu.with_memory_space_constraint(a, pltpu.HBM) for a in far]
    return pl.pallas_call(
        run,
        out_shape=tuple(pltpu.VMEM(shape, kind) for shape, kind in outs),
        in_specs=[SMEM] * len(lead) + [VMEM] * len(near) + [ANY] * len(far) + [VMEM] * len(past),
        out_specs=(VMEM,) * len(outs),
        scratch_shapes=list(scratch),
        input_output_aliases={len(lead) + i: o for i, o in (aliases or {}).items()},
        compiler_params=pltpu.CompilerParams(vmem_limit_bytes=grant << 20),
        cost_estimate=cost(flops, 0),
    )(*lead, *near, *far, *past)


def fill(xt_ref, x_ref, scale_ref, starts, r):
    scale = scale_ref[...]
    for j, at in enumerate(starts):
        piece = x_ref[:, pl.ds(pl.multiple_of(at, 128), r)].astype(F32) * scale
        xt_ref[j * r : (j + 1) * r, :] = piece.astype(jnp.bfloat16).T


def columns(side, cols, q, w):
    return slice(side * cols // 2 + q, side * cols // 2 + q + w)


def first_call(x, c, owners, n, rows, chunk):
    off, q, w = chunk
    r = ROWS
    tokens, width = x.shape
    cols = c.shape[1]
    half = n // 2
    tile = 256
    group = 64
    steps = tokens // tile
    parts = [columns(side, cols, q, w) for side in range(2)]
    others = [
        slice(lo, hi)
        for side in range(2)
        for lo, hi in ((side * cols // 2, parts[side].start), (parts[side].stop, (side + 1) * cols // 2))
        if lo < hi
    ]

    def kernel(own, x_hbm, c_hbm, x_ref, c_ref, s_ref, p_ref, xt_ref, xe_ref, x_sem, c_sem):
        def rows_at(i):
            return pl.ds(pl.multiple_of(i * tile, tile), tile)

        def piece(i):
            at = rows_at(i)
            return pltpu.make_async_copy(x_hbm.at[at, :], x_ref.at[at, :], x_sem.at[i])

        def begin(i, _):
            piece(i).start()
            return 0

        def scales(i):
            out = []
            for g in range(0, tile, group):
                at = pl.ds(pl.multiple_of(i * tile + g, group), group)
                total = jnp.zeros((group, 128), F32)
                for s in range(0, width, 128):
                    v = x_ref[at, s : s + 128].astype(F32)
                    total = total + v * v
                stat = jnp.sum(total, axis=1, keepdims=True) / width
                out.append(jnp.broadcast_to(lax.rsqrt(stat + EPS), (group, 128)))
            return jnp.concatenate(out, axis=0)

        def turn(i, now):
            at = rows_at(i)
            for parity, out in ((1, xt_ref), (0, xe_ref)):
                for j in range(half):
                    lanes = pl.ds(pl.multiple_of(own[2 * j + parity] * rows + off, 128), r)
                    value = (x_ref[at, lanes].astype(F32) * now).astype(jnp.bfloat16)
                    out[j * r : (j + 1) * r, at] = value.T

        def both(i, _):
            piece(i + 1).wait()
            now = s_ref[rows_at(i), :]
            later = scales(i + 1)
            turn(i, now)
            s_ref[rows_at(i + 1), :] = later
            return 0

        near = [
            pltpu.make_async_copy(c_hbm.at[:, at], c_ref.at[:, at], c_sem.at[k])
            for k, at in enumerate(parts + others)
        ]
        near, rest = near[:2], near[2:]
        for copy in near:
            copy.start()
        lax.fori_loop(0, steps, begin, 0)
        for copy in rest:
            copy.start()
        piece(0).wait()
        s_ref[rows_at(0), :] = scales(0)
        lax.fori_loop(0, steps - 2, both, 0)
        for copy in near:
            copy.wait()
        cut = (steps - 2) * tile
        for side in range(2):
            p_ref[:, :, side * w : (side + 1) * w] = jnp.dot(
                xt_ref[:, :cut], c_ref[:cut, parts[side]], preferred_element_type=F32
            ).reshape(half, r, w)
        both(steps - 2, 0)
        turn(steps - 1, s_ref[rows_at(steps - 1), :])
        for side in range(2):
            p_ref[:, :, side * w : (side + 1) * w] += jnp.dot(
                xt_ref[:, cut:], c_ref[cut:, parts[side]], preferred_element_type=F32
            ).reshape(half, r, w)
        for copy in rest:
            copy.wait()

    return pl.pallas_call(
        kernel,
        out_shape=(
            pltpu.VMEM(x.shape, x.dtype),
            pltpu.VMEM(c.shape, c.dtype),
            pltpu.VMEM((tokens, 128), F32),
            pltpu.VMEM((half, r, 2 * w), F32),
            pltpu.VMEM((half * r, tokens), jnp.bfloat16),
            pltpu.VMEM((half * r, tokens), jnp.bfloat16),
        ),
        in_specs=[SMEM, ANY, ANY],
        out_specs=(VMEM,) * 6,
        scratch_shapes=[
            pltpu.SemaphoreType.DMA((steps,)),
            pltpu.SemaphoreType.DMA((2 + len(others),)),
        ],
        compiler_params=pltpu.CompilerParams(vmem_limit_bytes=12 << 20),
        cost_estimate=cost(4 * tokens * half * r * w, 2 * tokens * (width + cols)),
        name="first",
    )(owners, *[pltpu.with_memory_space_constraint(a, pltpu.HBM) for a in (x, c)])


def product_call(x, scale, c, owners, n, rows, chunk, parity, xt, tokens):
    off, q, w = chunk
    r = ROWS
    cols = c.shape[1]
    half = n // 2

    def multiply(xt_ref, c_ref, out_ref):
        for side in range(2):
            out_ref[:, :, side * w : (side + 1) * w] = jnp.dot(
                xt_ref[...], c_ref[:, columns(side, cols, q, w)], preferred_element_type=F32
            ).reshape(half, r, w)

    def kernel(own, x_ref, s_ref, c_ref, out_ref, xt_ref):
        fill(xt_ref, x_ref, s_ref, [own[2 * j + parity] * rows + off for j in range(half)], r)
        multiply(xt_ref, c_ref, out_ref)

    shape = (half, r, 2 * w)
    flops = 4 * x.shape[0] * half * r * w
    if xt is not None:
        (out,) = on_chip(multiply, [xt, c], tokens, [shape], flops=flops)
        return out, xt
    return on_chip(
        kernel, [x, scale, c], tokens,
        [shape, ((half * r, x.shape[0]), jnp.bfloat16)], owners=owners, flops=flops,
    )


def part_call(even, got, sends, keeps, tokens):
    r, w = even.shape[1], even.shape[2] // 2

    def kernel(even_ref, got_ref, *outs):
        for side in range(2):
            at = slice(side * w, (side + 1) * w)
            for out, masks in ((outs[2 * side], sends[side]), (outs[2 * side + 1], keeps[side])):
                for k, m in enumerate(masks):
                    out[k] = even_ref[m // 2, :, at] + got_ref[m // 2, :, at]

    shapes = [(len(m), r, w) for side in range(2) for m in (sends[side], keeps[side])]
    return on_chip(kernel, [even, got], tokens, shapes)


def add_up(terms, refs):
    total = None
    for array, at in terms:
        value = refs[array][at]
        total = value if total is None else total + value
    return total


def gather(groups):
    arrays, places = [], {}

    def place(array):
        if id(array) not in places:
            places[id(array)] = len(arrays)
            arrays.append(array)
        return places[id(array)]

    plan = [[[(place(a), at) for a, at in terms] for terms in group] for group in groups]
    return arrays, plan


def stage_call(sends, r, wide, tokens):
    arrays, plan = gather(sends)

    def kernel(*refs):
        for out, group in zip(refs[len(arrays) :], plan):
            for j, terms in enumerate(group):
                out[j] = add_up(terms, refs)

    return on_chip(kernel, arrays, tokens, [(len(g), r, wide) for g in plan])


def last_call(sends, keeps, momentum, consts, chunks, rows, wide, before, tokens):
    arrays, plan = gather([sends, keeps])
    terms = len(arrays)
    r = ROWS
    off, _, w = chunks[0]
    narrow = wide * BAND // CH
    low = r * BAND // CH
    high = rows * BAND // CH
    arrays = arrays + [momentum, consts["bands_left"], consts["bands_right"]]
    aliases = {}
    for k, array in enumerate(before or []):
        aliases[len(arrays)] = 2 + k
        arrays.append(array)
    count = len(arrays)
    subs = len(chunks)

    def kernel(*refs):
        out_refs = refs[count : count + 2]
        l_ref, ba_ref, bb_ref, bl_ref = refs[count + 2 :]
        m_ref, left_ref, right_ref = refs[terms : terms + 3]
        sums = [add_up(t, refs) for group in plan for t in group]
        for side in range(2):
            for k, (_, q, _) in enumerate(chunks):
                out_refs[side][k] = sums[side * subs + k]
                at = columns(side, 2 * wide, q, w)
                mine = sums[(2 + side) * subs + k] + momentum_decay * m_ref[0, off : off + r, at]
                sums[(2 + side) * subs + k] = mine
                l_ref[off : off + r, at] = mine
        fields = [total[:, s : s + SPAN] for total in sums for s in range(0, w, SPAN)]
        bands = bands_of(fields, left_ref[...], right_ref[...])
        at = slice(off * BAND // CH, off * BAND // CH + low)
        ba_ref[at, :] = bands[:, :narrow]
        bb_ref[at, :] = bands[:, narrow : 2 * narrow]
        bl_ref[at, :] = bands[:, 2 * narrow :]

    shapes = [
        (subs, r, w), (subs, r, w), (rows, 2 * wide),
        (high, narrow), (high, narrow), (high, 2 * narrow),
    ]
    return on_chip(kernel, arrays, tokens, shapes, flops=24 * r * wide * 128, aliases=aliases)


def join_call(own, a, b):
    narrow = a.shape[1]

    def kernel(own_ref, a_ref, b_ref, out_ref):
        out_ref[:, :narrow] = own_ref[:, :narrow] + a_ref[...]
        out_ref[:, narrow:] = own_ref[:, narrow:] + b_ref[...]

    return on_chip(kernel, [own, a, b], [], [own.shape])[0]


def tree(terms):
    while len(terms) > 1:
        terms = [terms[k] + terms[k + 1] for k in range(0, len(terms), 2)]
    return terms[0]


def outward(kernel, ins, tokens, shape, parts, part, flops, before=None):
    olds = [] if before is None else [before]

    def run(*refs):
        lead = refs[: len(ins)]
        out_hbm, buf, sem = refs[len(ins) + len(tokens) + len(olds) :]

        def send(k, index):
            pltpu.make_async_copy(buf.at[k], out_hbm.at[index], sem.at[k]).start()

        def wait(k, index):
            pltpu.make_async_copy(buf.at[k], out_hbm.at[index], sem.at[k]).wait()

        indices = kernel(buf, send, *lead)
        for k, index in enumerate(indices):
            wait(k, index)

    arrays = [pltpu.with_memory_space_constraint(a, pltpu.VMEM) for a in [*ins, *tokens]]
    return pl.pallas_call(
        run,
        out_shape=jax.ShapeDtypeStruct(shape, F32),
        in_specs=[VMEM] * len(arrays) + [ANY] * len(olds),
        out_specs=ANY,
        scratch_shapes=[pltpu.VMEM((parts,) + part, F32), pltpu.SemaphoreType.DMA((parts,))],
        input_output_aliases={len(arrays): 0} if olds else {},
        compiler_params=pltpu.CompilerParams(vmem_limit_bytes=12 << 20),
        cost_estimate=cost(flops, 4 * parts * part[0] * part[1]),
    )(*arrays, *olds)


def update_call(bands, consts, rows, cols, tokens):
    count = len(bands)
    parts = rows // ROWS

    def kernel(buf, send, *refs):
        total = tree([ref[...] for ref in refs[:count]]) / count
        pieces = expand(total, refs[count][...], refs[count + 1][...])
        indices = [pl.ds(k * ROWS, ROWS) for k in range(parts)]
        for k, piece in enumerate(pieces):
            buf[k] = piece
            send(k, indices[k])
        return indices

    return outward(
        kernel, [*bands, consts["expand_left"], consts["expand_right"]], tokens,
        (rows, cols), parts, (ROWS, cols), 6 * rows * cols * 128,
    )


def settle_call(own, bands, consts, tokens):
    def kernel(own_ref, g_ref, left_ref, right_ref, out_ref):
        for k, taken in enumerate(expand(g_ref[...], left_ref[...], right_ref[...])):
            at = slice(k * ROWS, (k + 1) * ROWS)
            out_ref[at, :] = own_ref[at, :] - taken

    return on_chip(
        kernel, [own, bands, consts["expand_left"], consts["expand_right"]], tokens,
        [own.shape], flops=6 * own.size * 128, aliases={0: 0},
    )[0]


def finish_call(own, a, b, chunks, before, tokens):
    rows, cols = own.shape
    off, _, w = chunks[0]
    parts = 2
    step = ROWS // parts

    def kernel(buf, send, own_ref, a_ref, b_ref):
        indices = []
        for part in range(parts):
            lo = part * step
            for side, ref in enumerate((a_ref, b_ref)):
                for k, (_, q, _) in enumerate(chunks):
                    at = columns(side, cols, q, w)
                    buf[part, :, at] = own_ref[off + lo : off + lo + step, at] + ref[k, lo : lo + step]
            indices.append((0, pl.ds(off + lo, step)))
            send(part, indices[part])
        return indices

    return outward(kernel, [own, a, b], tokens, (1, rows, cols), parts, (step, cols), 0, before)


def chunks_of(rows, wide):
    offs = list(range(0, rows, ROWS))
    groups = []
    for k, off in enumerate(offs):
        w = wide // 2 if k < 2 else wide
        groups.append([(off, q, w) for q in range(0, wide, w)])
    return groups


def fast_body(n, groups, activations, cotangent, momentum):
    x, c = activations[0], cotangent[0]
    width = x.shape[1]
    cols = c.shape[1]
    rows = width // n
    wide = cols // 2
    consts = constants()
    owners = lax.axis_index("fsdp").astype(jnp.int32) ^ jnp.arange(n, dtype=jnp.int32)
    bits = [1 << b for b in range(1, n.bit_length() - 1)]
    orders = (bits, bits[::-1])
    evens = range(0, n, 2)
    sends = [[m for m in evens if m & order[0]] for order in orders]
    keeps = [[m for m in evens if not m & order[0]] for order in orders]

    def swap(value, bit, axis="fsdp", size=n):
        return lax.ppermute(value, axis, [(i, i ^ bit) for i in range(size)])

    row_groups = chunks_of(rows, wide)
    chunks = [chunk for group in row_groups for chunk in group]
    x, c, scale, odd, *xts = first_call(x, c, owners, n, rows, chunks[0])
    token = odd
    kept = {(1, chunks[0][0]): xts[0], (0, chunks[0][0]): xts[1]}

    def product(k, parity):
        at = parity, chunks[k][0]
        out, kept[at] = product_call(
            x, scale, c, owners, n, rows, chunks[k], parity, kept.get(at), [token]
        )
        return out

    got = swap(odd, 1)
    state = []
    for k, chunk in enumerate(chunks):
        even = product(k, 0)
        token = even
        here = got
        if k + 1 < len(chunks) and k + 1 not in LATE:
            odd = product(k + 1, 1)
            token = odd
            got = swap(odd, 1)
        outs = part_call(even, here, sends, keeps, [token])
        token = outs[1]
        if k + 1 < len(chunks) and k + 1 in LATE:
            odd = product(k + 1, 1)
            token = odd
            got = swap(odd, 1)
        terms = []
        for side in range(2):
            back = swap(outs[2 * side], orders[side][0])
            terms.append({m: [(outs[2 * side + 1], j), (back, j)] for j, m in enumerate(keeps[side])})
        for stage in range(1, len(bits) - 1):
            now = [orders[side][stage] for side in range(2)]
            out = stage_call(
                [[terms[side][m] for m in sorted(terms[side]) if m & now[side]] for side in range(2)],
                ROWS, chunk[2], [],
            )
            for side in range(2):
                back = swap(out[side], now[side])
                keep = [m for m in sorted(terms[side]) if not m & now[side]]
                terms[side] = {m: terms[side][m] + [(back, j)] for j, m in enumerate(keep)}
        state.append(terms)

    ends = [order[-1] for order in orders]
    before = None
    bulk = []
    at = 0
    for group in row_groups:
        held = state[at : at + len(group)]
        at += len(group)
        a, b, *before = last_call(
            [terms[side][ends[side]] for side in range(2) for terms in held],
            [terms[side][0] for side in range(2) for terms in held],
            momentum, consts, group, rows, wide, before, [token],
        )
        token = a
        bulk.append((swap(a, ends[0]), swap(b, ends[1])))
    band_a = swap(before[1], ends[0])
    band_b = swap(before[2], ends[1])
    mine = join_call(before[3], band_a, band_b)
    every = [mine] + [swap(mine, k, "rep", groups) for k in range(1, groups)]
    settled = settle_call(before[0], mine, consts, [])
    nexts = None
    final = len(row_groups) - 1
    for g, group in enumerate(row_groups):
        if g == final:
            update = update_call(every, consts, rows, cols, [settled])
        nexts = finish_call(settled, *bulk[g], group, nexts, [])
    return nexts, update


def plain_body(n, groups, activations, cotangent, momentum):
    values = activations[0].astype(jnp.float32)
    stat = jnp.mean(values * values, axis=-1, keepdims=True)
    normed = (values * lax.rsqrt(stat + EPS)).astype(jnp.bfloat16)
    part = lax.dot_general(
        normed, cotangent[0], (((0,), (0,)), ((), ())), preferred_element_type=jnp.float32
    )
    basis = jnp.asarray(basis_rows(CH, BAND))
    grad = lax.psum_scatter(part, "fsdp", scatter_dimension=0, tiled=True)
    accumulated = momentum_decay * momentum[0] + grad
    rows, width = accumulated.shape
    blocks = accumulated.reshape(rows // CH, CH, width // CH, CH)
    high = lax.Precision.HIGHEST
    bands = jnp.einsum("kn,anbm,lm->akbl", basis, blocks, basis, precision=high)
    own = jnp.einsum("kn,akbl,lm->anbm", basis, bands, basis, precision=high)
    summed = lax.psum(bands, "rep")
    every = jnp.einsum("kn,akbl,lm->anbm", basis, summed, basis, precision=high)
    return ((accumulated - own.reshape(rows, width))[None], every.reshape(rows, width) / groups)


def power(k):
    return k & (k - 1) == 0


def solution(mesh):
    n, groups = mesh.shape["fsdp"], mesh.shape["rep"]
    fits = power(n) and n >= 4 and power(groups)

    def body(activations, cotangent, momentum):
        rows, cols = momentum.shape[1:]
        good = fits and rows % ROWS == 0 and cols % (4 * SPAN) == 0 and activations.shape[1] % 512 == 0
        return (fast_body if good else plain_body)(n, groups, activations, cotangent, momentum)

    return jax.shard_map(
        body,
        mesh=mesh,
        in_specs=(P("rep", "fsdp", None), P("rep", "fsdp", None), P("rep", "fsdp", None)),
        out_specs=(P("rep", "fsdp", None), P("fsdp", None)),
        check_vma=False,
    )
```

```python
import jax
import jax.numpy as jnp
import numpy as np
from jax import lax
from jax.experimental import pallas as pl
from jax.experimental.pallas import tpu as pltpu
from jax.sharding import PartitionSpec as P

CH = 64
BAND = 16
EPS = 1e-05
ROWS = 128
SPAN = 256

momentum_decay = 0.9


def basis_rows(size, keep):
    freq = np.arange(keep, dtype=np.float64)[:, None]
    point = np.arange(size, dtype=np.float64)[None, :]
    waves = np.cos(np.pi * (2.0 * point + 1.0) * freq / (2.0 * size))
    scales = np.where(freq == 0.0, np.sqrt(1.0 / size), np.sqrt(2.0 / size))
    return (waves * scales).astype(np.float32)


def halves(value):
    high = value.astype(jnp.bfloat16)
    return high, (value - high.astype(jnp.float32)).astype(jnp.bfloat16)


def times_const(value, const):
    high, low = halves(value)
    return jnp.dot(
        jnp.concatenate([high, low, high], axis=1), const, preferred_element_type=jnp.float32
    )


def const_times(const, value):
    high, low = halves(value)
    return jnp.dot(
        const, jnp.concatenate([high, low, high], axis=0), preferred_element_type=jnp.float32
    )


def constants():
    small = basis_rows(CH, BAND)
    left = np.kron(np.eye(ROWS // CH, dtype=np.float32), small)
    right = np.kron(np.eye(SPAN // CH, dtype=np.float32), small.T)

    def split(m, axis):
        high, low = halves(jnp.asarray(m))
        parts = [high, high, low]
        return jnp.concatenate(parts, axis=axis)

    return {
        "bands_left": split(left, 1),
        "bands_right": split(right, 0),
        "expand_left": split(left.T, 1),
        "expand_right": split(right.T, 0),
    }


def bands_of(fields, left, right):
    tall = times_const(jnp.concatenate(fields, axis=0), right)
    wide = jnp.concatenate([tall[k * ROWS : (k + 1) * ROWS] for k in range(len(fields))], axis=1)
    return const_times(left, wide)


def expand(bands, left, right):
    low = ROWS * BAND // CH
    part = SPAN * BAND // CH
    spans = bands.shape[1] // part
    count = bands.shape[0]
    tall = times_const(
        jnp.concatenate([bands[:, s * part : (s + 1) * part] for s in range(spans)], axis=0), right
    )
    wide = jnp.concatenate([tall[s * count : (s + 1) * count] for s in range(spans)], axis=1)
    return [const_times(left, wide[k : k + low]) for k in range(0, count, low)]


def cost(flops, nbytes):
    return pl.CostEstimate(flops=int(flops), bytes_accessed=int(nbytes), transcendentals=0)


ANY = pl.BlockSpec(memory_space=pl.ANY)
VMEM = pl.BlockSpec(memory_space=pltpu.VMEM)
SMEM = pl.BlockSpec(memory_space=pltpu.SMEM)
F32 = jnp.float32


def on_chip(kernel, ins, tokens, outs, scratch=(), owners=None, flops=0, aliases=None, far=(), grant=12):
    lead = [] if owners is None else [owners]
    count = len(lead) + len(ins) + len(far)

    outs = [out if isinstance(out[0], tuple) else (out, F32) for out in outs]

    def run(*refs):
        kernel(*refs[:count], *refs[count + len(tokens) :])

    near = [pltpu.with_memory_space_constraint(a, pltpu.VMEM) for a in ins]
    past = [pltpu.with_memory_space_constraint(a, pltpu.VMEM) for a in tokens]
    far = [pltpu.with_memory_space_constraint(a, pltpu.HBM) for a in far]
    return pl.pallas_call(
        run,
        out_shape=tuple(pltpu.VMEM(shape, kind) for shape, kind in outs),
        in_specs=[SMEM] * len(lead) + [VMEM] * len(near) + [ANY] * len(far) + [VMEM] * len(past),
        out_specs=(VMEM,) * len(outs),
        scratch_shapes=list(scratch),
        input_output_aliases={len(lead) + i: o for i, o in (aliases or {}).items()},
        compiler_params=pltpu.CompilerParams(vmem_limit_bytes=grant << 20),
        cost_estimate=cost(flops, 0),
    )(*lead, *near, *far, *past)


def fill(xt_ref, x_ref, scale_ref, starts, r):
    scale = scale_ref[...]
    for j, at in enumerate(starts):
        piece = x_ref[:, pl.ds(pl.multiple_of(at, 128), r)].astype(F32) * scale
        xt_ref[j * r : (j + 1) * r, :] = piece.astype(jnp.bfloat16).T


def columns(side, cols, q, w):
    return slice(side * cols // 2 + q, side * cols // 2 + q + w)


def picked(xt_ref, masks, r, at=slice(None)):
    return jnp.concatenate([xt_ref[m // 2 * r : (m // 2 + 1) * r, at] for m in masks], axis=0)


def first_call(x, c, owners, n, rows, chunk, masks):
    off, q, w = chunk
    r = ROWS
    tokens, width = x.shape
    cols = c.shape[1]
    half = n // 2
    tile = 256
    group = 64
    steps = tokens // tile
    parts = [columns(side, cols, q, w) for side in range(2)]
    others = [
        slice(lo, hi)
        for side in range(2)
        for lo, hi in ((side * cols // 2, parts[side].start), (parts[side].stop, (side + 1) * cols // 2))
        if lo < hi
    ]

    def kernel(own, x_hbm, c_hbm, x_ref, c_ref, s_ref, p_ref, xt_ref, xe_ref, x_sem, c_sem):
        def rows_at(i):
            return pl.ds(pl.multiple_of(i * tile, tile), tile)

        def piece(i):
            at = rows_at(i)
            return pltpu.make_async_copy(x_hbm.at[at, :], x_ref.at[at, :], x_sem.at[i])

        def begin(i, _):
            piece(i).start()
            return 0

        def scales(i):
            out = []
            for g in range(0, tile, group):
                at = pl.ds(pl.multiple_of(i * tile + g, group), group)
                total = jnp.zeros((group, 128), F32)
                for s in range(0, width, 128):
                    v = x_ref[at, s : s + 128].astype(F32)
                    total = total + v * v
                stat = jnp.sum(total, axis=1, keepdims=True) / width
                out.append(jnp.broadcast_to(lax.rsqrt(stat + EPS), (group, 128)))
            return jnp.concatenate(out, axis=0)

        def turn(i, now):
            at = rows_at(i)
            for parity, out in ((1, xt_ref), (0, xe_ref)):
                for j in range(half):
                    lanes = pl.ds(pl.multiple_of(own[2 * j + parity] * rows + off, 128), r)
                    value = (x_ref[at, lanes].astype(F32) * now).astype(jnp.bfloat16)
                    out[j * r : (j + 1) * r, at] = value.T

        def both(i, _):
            piece(i + 1).wait()
            now = s_ref[rows_at(i), :]
            later = scales(i + 1)
            turn(i, now)
            s_ref[rows_at(i + 1), :] = later
            return 0

        near = [
            pltpu.make_async_copy(c_hbm.at[:, at], c_ref.at[:, at], c_sem.at[k])
            for k, at in enumerate(parts + others)
        ]
        near, rest = near[:2], near[2:]
        for copy in near:
            copy.start()
        lax.fori_loop(0, steps, begin, 0)
        for copy in rest:
            copy.start()
        piece(0).wait()
        s_ref[rows_at(0), :] = scales(0)
        lax.fori_loop(0, steps - 2, both, 0)
        for copy in near:
            copy.wait()
        cut = (steps - 2) * tile
        for side in range(2):
            p_ref[:, :, side * w : (side + 1) * w] = jnp.dot(
                picked(xt_ref, masks[side], r, slice(0, cut)), c_ref[:cut, parts[side]],
                preferred_element_type=F32,
            ).reshape(-1, r, w)
        both(steps - 2, 0)
        turn(steps - 1, s_ref[rows_at(steps - 1), :])
        for side in range(2):
            p_ref[:, :, side * w : (side + 1) * w] += jnp.dot(
                picked(xt_ref, masks[side], r, slice(cut, tokens)), c_ref[cut:, parts[side]],
                preferred_element_type=F32,
            ).reshape(-1, r, w)
        for copy in rest:
            copy.wait()

    return pl.pallas_call(
        kernel,
        out_shape=(
            pltpu.VMEM(x.shape, x.dtype),
            pltpu.VMEM(c.shape, c.dtype),
            pltpu.VMEM((tokens, 128), F32),
            pltpu.VMEM((len(masks[0]), r, 2 * w), F32),
            pltpu.VMEM((half * r, tokens), jnp.bfloat16),
            pltpu.VMEM((half * r, tokens), jnp.bfloat16),
        ),
        in_specs=[SMEM, ANY, ANY],
        out_specs=(VMEM,) * 6,
        scratch_shapes=[
            pltpu.SemaphoreType.DMA((steps,)),
            pltpu.SemaphoreType.DMA((2 + len(others),)),
        ],
        compiler_params=pltpu.CompilerParams(vmem_limit_bytes=12 << 20),
        cost_estimate=cost(4 * tokens * half * r * w, 2 * tokens * (width + cols)),
        name="first",
    )(owners, *[pltpu.with_memory_space_constraint(a, pltpu.HBM) for a in (x, c)])


def product_call(x, scale, c, owners, n, rows, chunk, parity, masks, xt, tokens):
    off, q, w = chunk
    r = ROWS
    cols = c.shape[1]
    half = n // 2

    def multiply(xt_ref, c_ref, out_ref):
        for side in range(2):
            out_ref[:, :, side * w : (side + 1) * w] = jnp.dot(
                picked(xt_ref, masks[side], r), c_ref[:, columns(side, cols, q, w)],
                preferred_element_type=F32,
            ).reshape(-1, r, w)

    def kernel(own, x_ref, s_ref, c_ref, out_ref, xt_ref):
        fill(xt_ref, x_ref, s_ref, [own[2 * j + parity] * rows + off for j in range(half)], r)
        multiply(xt_ref, c_ref, out_ref)

    shape = (len(masks[0]), r, 2 * w)
    flops = 4 * x.shape[0] * len(masks[0]) * r * w
    if xt is not None:
        (out,) = on_chip(multiply, [xt, c], tokens, [shape], flops=flops)
        return out, xt
    return on_chip(
        kernel, [x, scale, c], tokens,
        [shape, ((half * r, x.shape[0]), jnp.bfloat16)], owners=owners, flops=flops,
    )


def part_call(even, got, picks, tokens):
    r, w = even.shape[1], even.shape[2] // 2

    def kernel(even_ref, got_ref, *outs):
        for side in range(2):
            at = slice(side * w, (side + 1) * w)
            for k, j in enumerate(picks[side]):
                outs[side][k] = even_ref[j, :, at] + got_ref[j, :, at]

    return on_chip(kernel, [even, got], tokens, [(len(pick), r, w) for pick in picks])


def add_up(terms, refs):
    total = None
    for array, at, lanes in terms:
        value = refs[array][at, :, lanes]
        total = value if total is None else total + value
    return total


def gather(groups):
    arrays, places = [], {}

    def place(array):
        if id(array) not in places:
            places[id(array)] = len(arrays)
            arrays.append(array)
        return places[id(array)]

    plan = [[[(place(a), *at) for a, *at in terms] for terms in group] for group in groups]
    return arrays, plan


def stage_call(sends, r, wide, tokens):
    arrays, plan = gather(sends)

    def kernel(*refs):
        for out, group in zip(refs[len(arrays) :], plan):
            for j, terms in enumerate(group):
                out[j] = add_up(terms, refs)

    return on_chip(kernel, arrays, tokens, [(len(g), r, wide) for g in plan])


def last_call(sends, keeps, momentum, consts, chunks, rows, wide, before, tokens):
    arrays, plan = gather([sends, keeps])
    terms = len(arrays)
    r = ROWS
    off, _, w = chunks[0]
    narrow = wide * BAND // CH
    low = r * BAND // CH
    high = rows * BAND // CH
    arrays = arrays + [momentum, consts["bands_left"], consts["bands_right"]]
    aliases = {}
    for k, array in enumerate(before or []):
        aliases[len(arrays)] = 2 + k
        arrays.append(array)
    count = len(arrays)
    subs = len(chunks)

    def kernel(*refs):
        out_refs = refs[count : count + 2]
        l_ref, ba_ref, bb_ref, bl_ref = refs[count + 2 :]
        m_ref, left_ref, right_ref = refs[terms : terms + 3]
        sums = [add_up(t, refs) for group in plan for t in group]
        for side in range(2):
            for k, (_, q, _) in enumerate(chunks):
                out_refs[side][k] = sums[side * subs + k]
                at = columns(side, 2 * wide, q, w)
                mine = sums[(2 + side) * subs + k] + momentum_decay * m_ref[0, off : off + r, at]
                sums[(2 + side) * subs + k] = mine
                l_ref[off : off + r, at] = mine
        fields = [total[:, s : s + SPAN] for total in sums for s in range(0, w, SPAN)]
        bands = bands_of(fields, left_ref[...], right_ref[...])
        at = slice(off * BAND // CH, off * BAND // CH + low)
        ba_ref[at, :] = bands[:, :narrow]
        bb_ref[at, :] = bands[:, narrow : 2 * narrow]
        bl_ref[at, :] = bands[:, 2 * narrow :]

    shapes = [
        (subs, r, w), (subs, r, w), (rows, 2 * wide),
        (high, narrow), (high, narrow), (high, 2 * narrow),
    ]
    return on_chip(kernel, arrays, tokens, shapes, flops=24 * r * wide * 128, aliases=aliases)


def join_call(own, a, b):
    narrow = a.shape[1]

    def kernel(own_ref, a_ref, b_ref, out_ref):
        out_ref[:, :narrow] = own_ref[:, :narrow] + a_ref[...]
        out_ref[:, narrow:] = own_ref[:, narrow:] + b_ref[...]

    return on_chip(kernel, [own, a, b], [], [own.shape])[0]


def tree(terms):
    while len(terms) > 1:
        terms = [terms[k] + terms[k + 1] for k in range(0, len(terms), 2)]
    return terms[0]


def outward(kernel, ins, tokens, shape, parts, part, flops, before=None):
    olds = [] if before is None else [before]

    def run(*refs):
        lead = refs[: len(ins)]
        out_hbm, buf, sem = refs[len(ins) + len(tokens) + len(olds) :]

        def send(k, index):
            pltpu.make_async_copy(buf.at[k], out_hbm.at[index], sem.at[k]).start()

        def wait(k, index):
            pltpu.make_async_copy(buf.at[k], out_hbm.at[index], sem.at[k]).wait()

        indices = kernel(buf, send, *lead)
        for k, index in enumerate(indices):
            wait(k, index)

    arrays = [pltpu.with_memory_space_constraint(a, pltpu.VMEM) for a in [*ins, *tokens]]
    return pl.pallas_call(
        run,
        out_shape=jax.ShapeDtypeStruct(shape, F32),
        in_specs=[VMEM] * len(arrays) + [ANY] * len(olds),
        out_specs=ANY,
        scratch_shapes=[pltpu.VMEM((parts,) + part, F32), pltpu.SemaphoreType.DMA((parts,))],
        input_output_aliases={len(arrays): 0} if olds else {},
        compiler_params=pltpu.CompilerParams(vmem_limit_bytes=12 << 20),
        cost_estimate=cost(flops, 4 * parts * part[0] * part[1]),
    )(*arrays, *olds)


def update_call(bands, consts, rows, cols, tokens):
    count = len(bands)
    parts = rows // ROWS

    def kernel(buf, send, *refs):
        total = tree([ref[...] for ref in refs[:count]]) / count
        pieces = expand(total, refs[count][...], refs[count + 1][...])
        indices = [pl.ds(k * ROWS, ROWS) for k in range(parts)]
        for k, piece in enumerate(pieces):
            buf[k] = piece
            send(k, indices[k])
        return indices

    return outward(
        kernel, [*bands, consts["expand_left"], consts["expand_right"]], tokens,
        (rows, cols), parts, (ROWS, cols), 6 * rows * cols * 128,
    )


def settle_call(own, bands, consts, tokens):
    def kernel(own_ref, g_ref, left_ref, right_ref, out_ref):
        for k, taken in enumerate(expand(g_ref[...], left_ref[...], right_ref[...])):
            at = slice(k * ROWS, (k + 1) * ROWS)
            out_ref[at, :] = own_ref[at, :] - taken

    return on_chip(
        kernel, [own, bands, consts["expand_left"], consts["expand_right"]], tokens,
        [own.shape], flops=6 * own.size * 128, aliases={0: 0},
    )[0]


def finish_call(own, a, b, chunks, before, tokens):
    rows, cols = own.shape
    off, _, w = chunks[0]
    parts = 2
    step = ROWS // parts

    def kernel(buf, send, own_ref, a_ref, b_ref):
        indices = []
        for part in range(parts):
            lo = part * step
            for side, ref in enumerate((a_ref, b_ref)):
                for k, (_, q, _) in enumerate(chunks):
                    at = columns(side, cols, q, w)
                    buf[part, :, at] = own_ref[off + lo : off + lo + step, at] + ref[k, lo : lo + step]
            indices.append((0, pl.ds(off + lo, step)))
            send(part, indices[part])
        return indices

    return outward(kernel, [own, a, b], tokens, (1, rows, cols), parts, (step, cols), 0, before)


def chunks_of(rows, wide):
    offs = list(range(0, rows, ROWS))
    groups = []
    for k, off in enumerate(offs):
        w = wide // 2 if k < 2 else wide
        groups.append([(off, q, w) for q in range(0, wide, w)])
    return groups


def fast_body(n, groups, activations, cotangent, momentum):
    x, c = activations[0], cotangent[0]
    width = x.shape[1]
    cols = c.shape[1]
    rows = width // n
    wide = cols // 2
    consts = constants()
    owners = lax.axis_index("fsdp").astype(jnp.int32) ^ jnp.arange(n, dtype=jnp.int32)
    bits = [1 << b for b in range(1, n.bit_length() - 1)]
    orders = (bits, bits[::-1])
    evens = range(0, n, 2)
    sends = [[m for m in evens if m & order[0]] for order in orders]
    keeps = [[m for m in evens if not m & order[0]] for order in orders]

    def swap(value, bit, axis="fsdp", size=n):
        return lax.ppermute(value, axis, [(i, i ^ bit) for i in range(size)])

    row_groups = chunks_of(rows, wide)
    chunks = [chunk for group in row_groups for chunk in group]
    x, c, scale, odd, *xts = first_call(x, c, owners, n, rows, chunks[0], sends)
    token = odd
    turned = {(1, chunks[0][0]): xts[0], (0, chunks[0][0]): xts[1]}

    def product(chunk, parity, masks):
        at = parity, chunk[0]
        out, turned[at] = product_call(
            x, scale, c, owners, n, rows, chunk, parity, masks, turned.get(at), [token]
        )
        return out

    def masks_of(chunk):
        return sends if chunk[2] < wide else [list(evens)] * 2

    got = swap(odd, 1)
    backs = []
    whole_of = {}
    for k, chunk in enumerate(chunks):
        even = product(chunk, 0, masks_of(chunk))
        token = even
        here = got
        if k + 1 < len(chunks):
            odd = product(chunks[k + 1], 1, masks_of(chunks[k + 1]))
            token = odd
            got = swap(odd, 1)
        outs = part_call(
            even, here,
            [[masks_of(chunk)[side].index(m) for m in sends[side]] for side in range(2)], [token],
        )
        token = outs[1]
        if chunk[2] == wide:
            whole_of[chunk[0]] = even, here
        backs.append([swap(outs[side], orders[side][0]) for side in range(2)])

    state = []
    first = 0
    for group in row_groups:
        off = group[0][0]
        full = (off, 0, wide)
        for parity in range(2):
            turned.pop((parity, off), None)
        held = masks_of(group[0])
        if off in whole_of:
            even, got = whole_of[off]
        else:
            held = keeps
            odd = product(full, 1, keeps)
            token = odd
            got = swap(odd, 1)
            even = product(full, 0, keeps)
            token = even
        for k, (_, q, w) in enumerate(group):
            terms = []
            for side in range(2):
                lanes = slice(side * wide + q, side * wide + q + w)
                back = backs[first + k][side]
                terms.append({
                    m: [
                        (even, held[side].index(m), lanes),
                        (got, held[side].index(m), lanes),
                        (back, j, slice(0, w)),
                    ]
                    for j, m in enumerate(keeps[side])
                })
            for stage in range(1, len(bits) - 1):
                now = [orders[side][stage] for side in range(2)]
                out = stage_call(
                    [[terms[side][m] for m in sorted(terms[side]) if m & now[side]] for side in range(2)],
                    ROWS, w, [],
                )
                for side in range(2):
                    back = swap(out[side], now[side])
                    keep = [m for m in sorted(terms[side]) if not m & now[side]]
                    terms[side] = {
                        m: terms[side][m] + [(back, j, slice(0, w))] for j, m in enumerate(keep)
                    }
            state.append(terms)
        first += len(group)

    ends = [order[-1] for order in orders]
    before = None
    bulk = []
    at = 0
    for group in row_groups:
        held = state[at : at + len(group)]
        at += len(group)
        a, b, *before = last_call(
            [terms[side][ends[side]] for side in range(2) for terms in held],
            [terms[side][0] for side in range(2) for terms in held],
            momentum, consts, group, rows, wide, before, [token],
        )
        token = a
        bulk.append((swap(a, ends[0]), swap(b, ends[1])))
    band_a = swap(before[1], ends[0])
    band_b = swap(before[2], ends[1])
    mine = join_call(before[3], band_a, band_b)
    every = [mine] + [swap(mine, k, "rep", groups) for k in range(1, groups)]
    settled = settle_call(before[0], mine, consts, [])
    nexts = None
    final = len(row_groups) - 1
    for g, group in enumerate(row_groups):
        if g == final:
            update = update_call(every, consts, rows, cols, [settled])
        nexts = finish_call(settled, *bulk[g], group, nexts, [])
    return nexts, update


def plain_body(n, groups, activations, cotangent, momentum):
    values = activations[0].astype(jnp.float32)
    stat = jnp.mean(values * values, axis=-1, keepdims=True)
    normed = (values * lax.rsqrt(stat + EPS)).astype(jnp.bfloat16)
    part = lax.dot_general(
        normed, cotangent[0], (((0,), (0,)), ((), ())), preferred_element_type=jnp.float32
    )
    basis = jnp.asarray(basis_rows(CH, BAND))
    grad = lax.psum_scatter(part, "fsdp", scatter_dimension=0, tiled=True)
    accumulated = momentum_decay * momentum[0] + grad
    rows, width = accumulated.shape
    blocks = accumulated.reshape(rows // CH, CH, width // CH, CH)
    high = lax.Precision.HIGHEST
    bands = jnp.einsum("kn,anbm,lm->akbl", basis, blocks, basis, precision=high)
    own = jnp.einsum("kn,akbl,lm->anbm", basis, bands, basis, precision=high)
    summed = lax.psum(bands, "rep")
    every = jnp.einsum("kn,akbl,lm->anbm", basis, summed, basis, precision=high)
    return ((accumulated - own.reshape(rows, width))[None], every.reshape(rows, width) / groups)


def power(k):
    return k & (k - 1) == 0


def solution(mesh):
    n, groups = mesh.shape["fsdp"], mesh.shape["rep"]
    fits = power(n) and n >= 4 and power(groups)

    def body(activations, cotangent, momentum):
        rows, cols = momentum.shape[1:]
        good = fits and rows % ROWS == 0 and cols % (4 * SPAN) == 0 and activations.shape[1] % 512 == 0
        return (fast_body if good else plain_body)(n, groups, activations, cotangent, momentum)

    return jax.shard_map(
        body,
        mesh=mesh,
        in_specs=(P("rep", "fsdp", None), P("rep", "fsdp", None), P("rep", "fsdp", None)),
        out_specs=(P("rep", "fsdp", None), P("fsdp", None)),
        check_vma=False,
    )
```
